32 devices in a mesh: rep: 8 (over y, x, core), shard: 4 (over z).
Axes of the slice: x: 2, y: 2, z: 4, core: 2. Of those that a mesh axis runs over, the one named last changes fastest.
Arguments:
- tokens: bfloat16 [8192, 640], P(('rep', 'shard')), may hold values from -6 to 6
- cotangent: bfloat16 [8192, 640], P(('rep', 'shard')), may hold values from -6 to 6
- seq_lengths: int32 [16], replicated, may hold values from 1 to 1024, 8192 in all
- w_query: bfloat16 [640, 1024], P('shard'), may hold values from -0.25 to 0.25
- w_key: bfloat16 [640, 256], P('shard'), may hold values from -0.25 to 0.25
- w_value: bfloat16 [640, 256], P('shard'), may hold values from -0.25 to 0.25
- w_out: bfloat16 [1024, 640], P('shard'), may hold values from -0.1875 to 0.1875
- w_gate: bfloat16 [640, 2048], P('shard'), may hold values from -0.25 to 0.25
- w_up: bfloat16 [640, 2048], P('shard'), may hold values from -0.25 to 0.25
- w_down: bfloat16 [2048, 640], P('shard'), may hold values from -0.125 to 0.125
- g_in: bfloat16 [640], P('shard'), may hold values from -0.3984375 to 0.3984375
- g_query: bfloat16 [256], P('shard'), may hold values from -0.3984375 to 0.3984375
- g_key: bfloat16 [256], P('shard'), may hold values from -0.3984375 to 0.3984375
- g_post: bfloat16 [640], P('shard'), may hold values from -0.3984375 to 0.3984375
- g_pre: bfloat16 [640], P('shard'), may hold values from -0.3984375 to 0.3984375
- g_ffn: bfloat16 [640], P('shard'), may hold values from -0.3984375 to 0.3984375
Outputs:
- block_out: bfloat16 [8192, 640], P(('rep', 'shard'))
- tokens_grad: bfloat16 [8192, 640], P(('rep', 'shard'))
- query_grad: float32 [640, 1024], P('shard')
- key_grad: float32 [640, 256], P('shard')
- value_grad: float32 [640, 256], P('shard')
- out_grad: float32 [1024, 640], P('shard')
- gate_grad: float32 [640, 2048], P('shard')
- up_grad: float32 [640, 2048], P('shard')
- down_grad: float32 [2048, 640], P('shard')
- in_gain_grad: float32 [640], P('shard')
- query_gain_grad: float32 [256], P('shard')
- key_gain_grad: float32 [256], P('shard')
- post_gain_grad: float32 [640], P('shard')
- pre_gain_grad: float32 [640], P('shard')
- ffn_gain_grad: float32 [640], P('shard')
The draws below stay inside these ranges and needn't reach their ends.
Inputs may be any that keep to these rules, and one draw needn't show every extreme that they name: `seq_lengths`: the sequences lie end to end and fill all 8192 tokens; the longest has exactly 1024.
All inputs are finite; a program needn't handle non-finite values.
Results may differ from the reference program's by a relative error of at most 0.024.
Values may be sent and summed in bfloat16 or wider, within the bound.
No kernel may reach another device: no remote copies, remote signals or barrier semaphores. Data moves between devices by JAX's collectives and lax.ppermute only.
A program may use at most 128 MiB of HBM per device.

```python
import math
import jax
import jax.numpy as jnp
import numpy as np
from jax import lax

D = 640
HEADS = 4
HEAD_DIM = 256
FF = 2048
WINDOW = 512
SEQ_MOST = 1024
QD = 1024
TOKENS = 8192
NSEQ = 16


def level_of(own_key, dims, split, smallest, top_value):
    factor_of = 1.0
    for dim, parts in split:
        heights = jax.random.uniform(jax.random.fold_in(jax.random.fold_in(own_key, 6), dim), (parts,), jnp.float32, smallest / len(split), top_value / len(split))
        factor_of = factor_of * jnp.repeat(jnp.exp(heights), dims[dim] // parts).reshape((-1,) + (1,) * (len(dims) - 1 - dim))
    return factor_of


def profile(number_of, total, limit, slope):
    weights = [(1 << 20) // math.isqrt(grade ** slope) + 1 for grade in range(2, number_of + 1)]
    surplus, given = total - limit - (number_of - 1), [1] * (number_of - 1)
    while surplus > 0:
        free = [i for i in range(number_of - 1) if given[i] < limit]
        mass, budget = sum([weights[i] for i in free]), surplus
        for i in free:
            extra = min(limit - given[i], max(1, budget * weights[i] // mass), surplus)
            given[i] = given[i] + extra
            surplus = surplus - extra
    return np.array([limit] + given)


def ragged_sizes(stream_key, amount, total, limit, lean):
    if amount == 2:
        one = jax.random.randint(stream_key, (), max(1, total - limit), min(limit, total - 1) + 1)
        return jnp.stack([one, total - one])
    sizes = jnp.asarray(profile(amount, total, limit, lean), jnp.int32)
    couples = (amount - 1) // 2
    donor, receiver = sizes[1:1 + 2 * couples:2], sizes[2:2 + 2 * couples:2]
    slack = jnp.minimum(donor - 1, limit - receiver)
    shifted = jax.random.randint(jax.random.fold_in(stream_key, 1), (couples,), 0, 1 << 20) % (slack + 1)
    sizes = sizes.at[1:1 + 2 * couples:2].set(donor - shifted).at[2:2 + 2 * couples:2].set(receiver + shifted)
    return sizes[jax.random.permutation(jax.random.fold_in(stream_key, 2), amount)]


def normal_values(key, extent, scale, limit, pieces=(), kind=jnp.bfloat16):
    entries = jax.random.normal(key, extent, jnp.float32) * scale
    if len(pieces) > 0:
        entries = level_of(key, extent, pieces, -0.22, 0.18) * entries
    return jnp.clip(entries, min=-limit, max=limit).astype(kind)


def setup_inputs(seed: int = 0) -> dict:
    key_of = jax.random.split(jax.random.key(seed), 17)
    return {
        "tokens": normal_values(key_of[0], (TOKENS, D), 1.0, 6.0, ((0, 32),)),
        "cotangent": normal_values(key_of[1], (TOKENS, D), 1.0, 6.0, ((0, 32),)),
        "seq_lengths": ragged_sizes(key_of[2], NSEQ, TOKENS, SEQ_MOST, 1).astype(jnp.int32),
        "w_query": normal_values(key_of[3], (D, QD), D ** -0.5, 0.25, ((0, 4),)),
        "w_key": normal_values(key_of[4], (D, HEAD_DIM), D ** -0.5, 0.25, ((0, 4),)),
        "w_value": normal_values(key_of[5], (D, HEAD_DIM), D ** -0.5, 0.25, ((0, 4),)),
        "w_out": normal_values(key_of[6], (QD, D), QD ** -0.5, 0.1875, ((0, 4),)),
        "w_gate": normal_values(key_of[7], (D, FF), D ** -0.5, 0.25, ((0, 4),)),
        "w_up": normal_values(key_of[8], (D, FF), D ** -0.5, 0.25, ((0, 4),)),
        "w_down": normal_values(key_of[9], (FF, D), FF ** -0.5, 0.125, ((0, 4),)),
        "g_in": jnp.clip(jax.random.uniform(key_of[10], (D,), jnp.float32, -0.3984375, 0.3984375) * level_of(key_of[10], (D,), ((0, 4),), -0.4, 0.0), -0.3984375, 0.3984375).astype(jnp.bfloat16),
        "g_query": jnp.clip(jax.random.uniform(key_of[11], (HEAD_DIM,), jnp.float32, -0.3984375, 0.3984375) * level_of(key_of[11], (HEAD_DIM,), ((0, 4),), -0.4, 0.0), -0.3984375, 0.3984375).astype(jnp.bfloat16),
        "g_key": jnp.clip(jax.random.uniform(key_of[12], (HEAD_DIM,), jnp.float32, -0.3984375, 0.3984375) * level_of(key_of[12], (HEAD_DIM,), ((0, 4),), -0.4, 0.0), -0.3984375, 0.3984375).astype(jnp.bfloat16),
        "g_post": jnp.clip(jax.random.uniform(key_of[13], (D,), jnp.float32, -0.3984375, 0.3984375) * level_of(key_of[13], (D,), ((0, 4),), -0.4, 0.0), -0.3984375, 0.3984375).astype(jnp.bfloat16),
        "g_pre": jnp.clip(jax.random.uniform(key_of[14], (D,), jnp.float32, -0.3984375, 0.3984375) * level_of(key_of[14], (D,), ((0, 4),), -0.4, 0.0), -0.3984375, 0.3984375).astype(jnp.bfloat16),
        "g_ffn": jnp.clip(jax.random.uniform(key_of[15], (D,), jnp.float32, -0.3984375, 0.3984375) * level_of(key_of[15], (D,), ((0, 4),), -0.4, 0.0), -0.3984375, 0.3984375).astype(jnp.bfloat16),
    }


@jax.custom_vjp
def low(v):
    return lax.optimization_barrier(v.astype(jnp.bfloat16)).astype(jnp.float32)

@jax.custom_vjp
def low_back(v):
    return v

def low_keep(v):
    return (low(v), None)

def low_pass(kept, grad):
    return (grad,)

def back_keep(v):
    return (v, None)

def back_low(kept, grad):
    return (low(grad),)
low.defvjp(low_keep, low_pass)
low_back.defvjp(back_keep, back_low)
EPS = 1e-06
NEGATIVE = -1e+30
HIGHEST = lax.Precision.HIGHEST

def product(left, right):
    return jnp.dot(left, right, precision=HIGHEST, preferred_element_type=jnp.float32)

def scaled(vector, scale_gain):
    inv_root = lax.rsqrt(lax.optimization_barrier(jnp.mean(vector * vector, axis=-1, keepdims=True)) + EPS)
    return vector * inv_root * (1.0 + scale_gain)

def places(glob_index, lengths):
    seq_ends = jnp.cumsum(lengths).astype(jnp.int32)
    before = seq_ends[None, :] <= glob_index[:, None]
    segment = lax.optimization_barrier(jnp.sum(before.astype(jnp.int32), axis=1)).astype(jnp.int32)
    seq_start = lax.optimization_barrier(jnp.sum(jnp.where(before, lengths[None, :], 0), axis=1)).astype(jnp.int32)
    return (segment, (glob_index - seq_start).astype(jnp.int32))

def turning(position, width):
    half_width = width // 2
    frequency = jnp.exp(jnp.arange(half_width, dtype=jnp.float32) * (-2.0 * math.log(10000.0) / width))
    angles = position.astype(jnp.float32)[:, None] * frequency[None, :]
    return (jnp.cos(angles), jnp.sin(angles))

def rotate(vector, cos_table, sin_table):
    half_width = vector.shape[-1] // 2
    first_half = vector[..., :half_width]
    second_half = vector[..., half_width:]
    return jnp.concatenate([first_half * cos_table - second_half * sin_table, second_half * cos_table + first_half * sin_table], axis=-1)

def softmax_rows(scores):
    row_max = lax.optimization_barrier(jnp.max(scores, axis=-1, keepdims=True))
    exponent = jnp.exp(scores - row_max)
    return exponent / lax.optimization_barrier(jnp.sum(exponent, axis=-1, keepdims=True))

def forward(tokens, w_query, w_key, w_value, w_out, w_gate, w_up, w_down, g_in, g_query, g_key, g_post, g_pre, g_ffn, cos_table, sin_table, segment, glob_index):
    tok_count = tokens.shape[0]
    normed = low(scaled(tokens, g_in))
    q_proj = low_back(product(normed, w_query)).reshape(tok_count, HEADS, HEAD_DIM)
    k_proj = low_back(product(normed, w_key))
    values = low(low_back(product(normed, w_value)))
    queries = low(rotate(scaled(q_proj, g_query), cos_table[:, None, :], sin_table[:, None, :]))
    key_rows = low(rotate(scaled(k_proj, g_key), cos_table, sin_table))
    key_pad = jnp.concatenate([jnp.zeros((WINDOW, HEAD_DIM), jnp.float32), key_rows], axis=0)
    value_pad = jnp.concatenate([jnp.zeros((WINDOW, HEAD_DIM), jnp.float32), values], axis=0)
    seg_pad = jnp.concatenate([jnp.full((WINDOW,), -1, jnp.int32), segment], axis=0)
    glob_pad = jnp.concatenate([jnp.arange(-WINDOW, 0, dtype=jnp.int32), glob_index], axis=0)

    def attend_block(block_idx):
        row_start = (block_idx * WINDOW).astype(jnp.int32)
        query_rows = lax.dynamic_slice_in_dim(queries, row_start, WINDOW, 0).reshape(WINDOW * HEADS, HEAD_DIM)
        seg_query = lax.dynamic_slice_in_dim(segment, row_start, WINDOW, 0)
        glob_query = lax.dynamic_slice_in_dim(glob_index, row_start, WINDOW, 0)
        block_keys = lax.dynamic_slice_in_dim(key_pad, row_start, 2 * WINDOW, 0)
        block_values = lax.dynamic_slice_in_dim(value_pad, row_start, 2 * WINDOW, 0)
        seg_key = lax.dynamic_slice_in_dim(seg_pad, row_start, 2 * WINDOW, 0)
        glob_key = lax.dynamic_slice_in_dim(glob_pad, row_start, 2 * WINDOW, 0)
        allowed = (seg_key[None, :] == seg_query[:, None]) & (glob_key[None, :] <= glob_query[:, None]) & (glob_query[:, None] - glob_key[None, :] < WINDOW)
        allowed = jnp.repeat(allowed, HEADS, axis=0)
        scores = low_back(product(query_rows, block_keys.T) * HEAD_DIM ** (-0.5))
        scores = jnp.where(allowed, scores, NEGATIVE)
        attn_probs = low(softmax_rows(scores))
        return product(attn_probs, block_values)
    attended = lax.map(jax.checkpoint(attend_block), jnp.arange(TOKENS // WINDOW, dtype=jnp.int32))
    attended = low(low_back(attended.reshape(tok_count, HEADS * HEAD_DIM)))
    attn_proj = low_back(product(attended, w_out))
    residual = tokens + scaled(attn_proj, g_post)
    normed_two = low(scaled(residual, g_pre))
    gate_proj = low_back(product(normed_two, w_gate))
    up_proj = low_back(product(normed_two, w_up))
    mixed_act = low(jax.nn.gelu(gate_proj, approximate=True) * up_proj)
    ffn_proj = low_back(product(mixed_act, w_down))
    return residual + scaled(ffn_proj, g_ffn)

def reference(tokens, cotangent, seq_lengths, w_query, w_key, w_value, w_out, w_gate, w_up, w_down, g_in, g_query, g_key, g_post, g_pre, g_ffn):
    glob_index = jnp.arange(TOKENS, dtype=jnp.int32)
    segment, position = places(glob_index, seq_lengths)
    cos_table, sin_table = turning(position, HEAD_DIM)
    floats = tuple((array_in.astype(jnp.float32) for array_in in (tokens, w_query, w_key, w_value, w_out, w_gate, w_up, w_down, g_in, g_query, g_key, g_post, g_pre, g_ffn)))

    def layer_fn(*inputs):
        return forward(*inputs, cos_table, sin_table, segment, glob_index)
    result, pullback = jax.vjp(layer_fn, *floats)
    gradients = pullback(cotangent.astype(jnp.float32))
    return (result.astype(jnp.bfloat16), gradients[0].astype(jnp.bfloat16), gradients[1], gradients[2], gradients[3], gradients[4], gradients[5], gradients[6], gradients[7], gradients[8], gradients[9], gradients[10], gradients[11], gradients[12], gradients[13])
```

```python
import math

import jax
import jax.numpy as jnp
from jax import lax
from jax.sharding import PartitionSpec as P

HEADS = 4
HEAD_DIM = 256
WINDOW = 512
EPS = 1e-06
NEGATIVE = -1e30
ALL = ("rep", "shard")
LOW = jnp.bfloat16
F32 = jnp.float32


class Grid:
    def __init__(self):
        reps = lax.axis_size("rep")
        self.depth = lax.axis_size("shard")
        self.side = math.isqrt(reps // 2)
        assert 2 * self.side * self.side == reps
        rep = lax.axis_index("rep")
        self.z = lax.axis_index("shard")
        self.core = rep % 2
        col = (rep // 2) % self.side
        row = rep // (2 * self.side)
        self.first = jnp.where(self.core == 0, col, row)
        self.second = jnp.where(self.core == 0, row, col)
        self.place = self.second * self.side + self.first

    def pairs(self, move):
        side, depth = self.side, self.depth
        found = []
        for y in range(side):
            for x in range(side):
                for c in range(2):
                    for z in range(depth):
                        ty, tx, tc, tz = move(y, x, c, z)
                        source = ((y * side + x) * 2 + c) * depth + z
                        found.append((source, ((ty * side + tx) * 2 + tc) * depth + tz))
        return found

    def over_first(self, array, by):
        n = self.side
        return lax.ppermute(
            array,
            ALL,
            self.pairs(
                lambda y, x, c, z: (y, (x - by) % n, c, z) if c == 0 else ((y - by) % n, x, c, z)
            ),
        )

    def over_second(self, array, by):
        n = self.side
        return lax.ppermute(
            array,
            ALL,
            self.pairs(
                lambda y, x, c, z: ((y - by) % n, x, c, z) if c == 0 else (y, (x - by) % n, c, z)
            ),
        )

    def over_depth(self, array, by):
        return lax.ppermute(
            array, ALL, self.pairs(lambda y, x, c, z: (y, x, c, (z - by) % self.depth))
        )

    def over_core(self, array):
        return lax.ppermute(array, ALL, self.pairs(lambda y, x, c, z: (y, x, 1 - c, z)))


def in_order(parts, index):
    n = len(parts)
    if n == 1:
        return list(parts)
    if n == 2:
        own, other = parts
        return [jnp.where(index == 0, own, other), jnp.where(index == 0, other, own)]
    rolled = jnp.roll(jnp.stack(parts), index, axis=0)
    return [rolled[i] for i in range(n)]


def place_shards(parts, z):
    n = len(parts)
    branches = [
        (lambda *a, s=s: jnp.concatenate([a[(m - s) % n] for m in range(n)], axis=0))
        for s in range(n)
    ]
    return lax.switch(z, branches, *parts)


def gather_plane(grid, block):
    n = grid.side
    line = jnp.stack(
        in_order([block] + [grid.over_first(block, k) for k in range(1, n)], grid.first)
    )
    return jnp.stack(
        in_order([line] + [grid.over_second(line, k) for k in range(1, n)], grid.second)
    )


def gather_core(grid, half):
    return in_order([half, grid.over_core(half)], grid.core)


def take(array, index, axis):
    return lax.dynamic_index_in_dim(array, index, axis, keepdims=False)


def add_low(a, *others):
    total = a.astype(F32)
    for b in others:
        total = total + b.astype(F32)
    return total


def reduce_plane(grid, keep, send, extra=None):
    n = grid.side
    total = add_low(keep, grid.over_core(send)).astype(LOW)
    got = [
        grid.over_first(take(total, (grid.first - k) % n, 2), k) for k in range(1, n)
    ]
    total = add_low(take(total, grid.first, 2), *got).astype(LOW)
    got = [
        grid.over_second(take(total, (grid.second - k) % n, 1), k) for k in range(1, n)
    ]
    return add_low(take(total, grid.second, 1), *got).astype(LOW)


def reduce_depth(grid, total):
    n = grid.depth
    got = [grid.over_depth(take(total, (grid.z - k) % n, 0), k) for k in range(1, n)]
    return add_low(take(total, grid.z, 0), *got)


def shifted(array, by):
    peers = lax.axis_size(ALL)
    pairs = [(i, i + by) for i in range(peers) if 0 <= i + by < peers]
    return lax.ppermute(array, ALL, pairs)


def scaled(vector, scale_gain):
    inv_root = lax.rsqrt(jnp.mean(vector * vector, axis=-1, keepdims=True) + EPS)
    return vector * inv_root * (1.0 + scale_gain)


def places(glob_index, lengths):
    seq_ends = jnp.sum(
        jnp.where(
            jnp.arange(lengths.shape[0])[:, None] >= jnp.arange(lengths.shape[0])[None, :],
            lengths[None, :],
            0,
        ),
        axis=1,
    )
    before = seq_ends[None, :] <= glob_index[:, None]
    segment = jnp.sum(before.astype(jnp.int32), axis=1)
    seq_start = jnp.sum(jnp.where(before, lengths[None, :], 0), axis=1)
    return (segment, glob_index - seq_start)


def turning(position, width):
    half_width = width // 2
    frequency = jnp.exp(
        jnp.arange(half_width, dtype=F32) * (-2.0 * math.log(10000.0) / width)
    )
    angles = position.astype(F32)[:, None] * frequency[None, :]
    return (jnp.cos(angles), jnp.sin(angles))


def rotate(vector, cos_table, sin_table):
    half_width = vector.shape[-1] // 2
    first_half = vector[..., :half_width]
    second_half = vector[..., half_width:]
    return jnp.concatenate(
        [
            first_half * cos_table - second_half * sin_table,
            second_half * cos_table + first_half * sin_table,
        ],
        axis=-1,
    )


def geglu(gate_proj, up_proj):
    return jax.nn.gelu(gate_proj, approximate=True) * up_proj


def matmul(left, right, pattern):
    return jnp.einsum(pattern, left, right, preferred_element_type=F32)


def attend_scores(queries, key_all, allowed):
    scores = matmul(queries, key_all, "qd,kd->qk") * HEAD_DIM ** (-0.5)
    return jnp.where(allowed, scores, NEGATIVE)


def local(
    tokens,
    cotangent,
    seq_lengths,
    w_query,
    w_key,
    w_value,
    w_out,
    w_gate,
    w_up,
    w_down,
    g_in,
    g_query,
    g_key,
    g_post,
    g_pre,
    g_ffn,
):
    grid = Grid()
    depth, side = grid.depth, grid.side
    spots = side * side
    tok_rows, width = tokens.shape
    rows = w_query.shape[0]
    half = rows // 2
    qd, kd = w_query.shape[1], w_key.shape[1]
    out_rows, down_rows, ff = w_out.shape[0], w_down.shape[0], w_gate.shape[1]
    proj_cols = (qd + 2 * kd) // spots
    ff_cols = ff // spots
    out_part, down_part = out_rows // (2 * spots), down_rows // (2 * spots)

    near_tok = shifted(tokens, 1)
    far_tok = shifted(tokens, 2)

    w_proj = jnp.concatenate([w_query, w_key, w_value], axis=1)
    gains_own = jnp.concatenate([g_in, g_post, g_pre, g_ffn, g_query, g_key])
    gain_len = gains_own.shape[0]
    proj_mine = lax.dynamic_slice(
        w_proj, (grid.core * half, grid.place * proj_cols), (half, proj_cols)
    )
    gain_rows = -(-gain_len // (proj_cols * 16)) * 16
    gain_block = jnp.pad(gains_own, (0, gain_rows * proj_cols - gain_len)).reshape(
        gain_rows, proj_cols
    )
    row_mine = jnp.concatenate(
        [
            lax.dynamic_slice_in_dim(
                w_out, (grid.core * spots + grid.place) * out_part, out_part, 0
            ),
            lax.dynamic_slice_in_dim(
                w_down, (grid.core * spots + grid.place) * down_part, down_part, 0
            ),
        ],
        axis=0,
    )
    pair_mine = jnp.concatenate(
        [
            lax.dynamic_slice(w, (grid.core * half, grid.place * ff_cols), (half, ff_cols))
            for w in (w_gate, w_up)
        ],
        axis=1,
    )

    proj_sent = jnp.concatenate([proj_mine, gain_block], axis=0)
    proj_got = [grid.over_depth(proj_sent, k) for k in range(1, depth)]
    row_got = [grid.over_depth(row_mine, k) for k in range(1, depth)]
    pair_got = [grid.over_depth(pair_mine, k) for k in range(1, depth)]

    gains_all = place_shards(
        [gain_block[None]] + [g[None, half:] for g in proj_got], grid.z
    ).reshape(depth, -1)[:, :gain_len].astype(F32)
    gain_sizes = [g.shape[0] for g in (g_in, g_post, g_pre, g_ffn, g_query, g_key)]
    gain_starts = [sum(gain_sizes[:i]) for i in range(len(gain_sizes))]
    gain_in, gain_post, gain_pre, gain_ffn, gain_query, gain_key = [
        gains_all[:, s : s + n].reshape(-1) for s, n in zip(gain_starts, gain_sizes)
    ]

    proj_halves = gather_core(
        grid, gather_plane(grid, jnp.stack([g[:half] for g in proj_got]))
    )
    proj_parts = jnp.stack(proj_halves).transpose(3, 0, 4, 1, 2, 5)
    proj_parts = proj_parts.reshape(depth - 1, rows, qd + 2 * kd)
    proj_full = place_shards(
        [w_proj[None]] + [proj_parts[k : k + 1] for k in range(depth - 1)], grid.z
    ).reshape(depth * rows, qd + 2 * kd)

    row_halves = jnp.stack(gather_core(grid, gather_plane(grid, jnp.stack(row_got))))
    row_halves = row_halves.transpose(3, 0, 1, 2, 4, 5).reshape(
        depth - 1, 2, spots, out_part + down_part, width
    )
    out_parts = row_halves[:, :, :, :out_part].reshape(depth - 1, out_rows, width)
    down_parts = row_halves[:, :, :, out_part:].reshape(depth - 1, down_rows, width)
    out_full = place_shards(
        [w_out[None]] + [out_parts[k : k + 1] for k in range(depth - 1)], grid.z
    ).reshape(depth * out_rows, width)
    down_full = place_shards(
        [w_down[None]] + [down_parts[k : k + 1] for k in range(depth - 1)], grid.z
    ).reshape(depth * down_rows, width)

    pair_own = jnp.stack(
        [w_gate.reshape(rows, spots, ff_cols), w_up.reshape(rows, spots, ff_cols)], axis=2
    ).reshape(rows, 2 * ff)
    pair_parts = jnp.stack(gather_core(grid, gather_plane(grid, jnp.stack(pair_got))))
    pair_parts = pair_parts.transpose(3, 0, 4, 1, 2, 5).reshape(depth - 1, rows, 2 * ff)
    pair_full = place_shards(
        [pair_own[None]] + [pair_parts[k : k + 1] for k in range(depth - 1)], grid.z
    ).reshape(depth * rows, 2 * ff)

    device = lax.axis_index(ALL)
    glob_index = device * tok_rows + jnp.arange(-2 * tok_rows, tok_rows, dtype=jnp.int32)
    segment, position = places(glob_index, seq_lengths)
    own_glob = glob_index[2 * tok_rows :]
    own_seg = segment[2 * tok_rows :]
    cos_all, sin_all = turning(position, HEAD_DIM)
    cos_table, sin_table = cos_all[2 * tok_rows :], sin_all[2 * tok_rows :]
    allowed = (
        (segment[None, :] == own_seg[:, None])
        & (glob_index[None, :] <= own_glob[:, None])
        & (own_glob[:, None] - glob_index[None, :] < WINDOW)
        & (glob_index[None, :] >= 0)
    )
    allowed = jnp.repeat(allowed, HEADS, axis=0)

    def query_side(q_proj, scale_gain):
        return rotate(
            scaled(q_proj.reshape(tok_rows, HEADS, HEAD_DIM), scale_gain),
            cos_table[:, None, :],
            sin_table[:, None, :],
        )

    def key_side(k_proj, scale_gain):
        return rotate(scaled(k_proj, scale_gain), cos_table, sin_table)

    tok_float = tokens.astype(F32)
    normed, in_pull = jax.vjp(scaled, tok_float, gain_in)
    normed_low = normed.astype(LOW)
    halo = jnp.concatenate([far_tok, near_tok], axis=0).astype(F32)
    halo_low = scaled(halo, gain_in).astype(LOW)
    proj_own = matmul(normed_low, proj_full, "tc,cq->tq")
    q_proj = proj_own[:, :qd]
    k_proj = proj_own[:, qd : qd + kd]
    v_proj = proj_own[:, qd + kd :]
    halo_proj = matmul(halo_low, proj_full[:, qd:], "tc,cq->tq")
    halo_keys = rotate(
        scaled(halo_proj[:, :kd], gain_key), cos_all[: 2 * tok_rows], sin_all[: 2 * tok_rows]
    )
    query_val, query_pull = jax.vjp(query_side, q_proj, gain_query)
    queries = query_val.astype(LOW).reshape(tok_rows * HEADS, HEAD_DIM)
    key_val, key_pull = jax.vjp(key_side, k_proj, gain_key)
    key_all = jnp.concatenate([halo_keys, key_val], axis=0).astype(LOW)
    value_all = jnp.concatenate([halo_proj[:, kd:], v_proj], axis=0).astype(LOW)
    scores = attend_scores(queries, key_all, allowed)
    row_max = jnp.max(scores, axis=-1, keepdims=True)
    exponent = jnp.exp(scores - row_max)
    row_total = jnp.sum(exponent, axis=-1, keepdims=True)
    attn_probs = exponent / row_total
    log_total = row_max + jnp.log(row_total)
    attended = matmul(attn_probs.astype(LOW), value_all, "qk,kd->qd")
    attended_low = attended.reshape(tok_rows, HEADS * HEAD_DIM).astype(LOW)
    attn_proj = matmul(attended_low, out_full, "tq,qc->tc")
    post_val, post_pull = jax.vjp(scaled, attn_proj, gain_post)
    residual = tok_float + post_val
    pre_val, pre_pull = jax.vjp(scaled, residual, gain_pre)
    normed_two = pre_val.astype(LOW)
    both = matmul(normed_two, pair_full, "tc,cf->tf").reshape(tok_rows, spots, 2, ff_cols)
    gate_proj, up_proj = both[:, :, 0], both[:, :, 1]
    mixed_val, mixed_pull = jax.vjp(geglu, gate_proj, up_proj)
    mixed_low = mixed_val.astype(LOW).reshape(tok_rows, ff)
    ffn_proj = matmul(mixed_low, down_full, "tf,fc->tc")
    ffn_val, ffn_pull = jax.vjp(scaled, ffn_proj, gain_ffn)
    block_out = (residual + ffn_val).astype(LOW)

    def halves(array, part):
        split = array.reshape(tok_rows, depth, 2, part)
        keep = take(split, grid.core, 2).reshape(tok_rows, depth * part)
        send = take(split, 1 - grid.core, 2).reshape(tok_rows, depth * part)
        return keep, send

    upstream = cotangent.astype(F32)
    d_ffn_proj, d_gain_ffn = ffn_pull(upstream)
    d_ffn_low = d_ffn_proj.astype(LOW)
    mixed_keep, mixed_send = halves(mixed_low, down_part * spots)
    grad_down = [matmul(m, d_ffn_low, "tf,tc->fc").astype(LOW) for m in (mixed_keep, mixed_send)]
    d_mixed = matmul(d_ffn_low, down_full, "tc,fc->tf").reshape(tok_rows, spots, ff_cols)
    d_gate, d_up = mixed_pull(d_mixed)
    d_both = jnp.stack([d_gate.astype(LOW), d_up.astype(LOW)], axis=2).reshape(tok_rows, 2 * ff)
    two_keep, two_send = halves(normed_two, half)
    grad_pair = [matmul(m, d_both, "tc,tf->cf").astype(LOW) for m in (two_keep, two_send)]
    d_normed_two = matmul(d_both, pair_full, "tf,cf->tc")
    d_resid_part, d_gain_pre = pre_pull(d_normed_two)
    d_residual = upstream + d_resid_part
    d_attn_proj, d_gain_post = post_pull(d_residual)
    d_attn_low = d_attn_proj.astype(LOW)
    att_keep, att_send = halves(attended_low, out_part * spots)
    grad_out = [matmul(m, d_attn_low, "tq,tc->qc").astype(LOW) for m in (att_keep, att_send)]

    pair_keep, pair_send = [
        g.reshape(depth, half, side, side, 2 * ff_cols).transpose(0, 2, 3, 1, 4)
        for g in grad_pair
    ]
    pair_sum = reduce_depth(grid, reduce_plane(grid, pair_keep, pair_send))
    row_keep, row_send = [
        jnp.concatenate(
            [
                o.reshape(depth, side, side, out_part, width),
                d.reshape(depth, side, side, down_part, width),
            ],
            axis=3,
        )
        for o, d in zip(grad_out, grad_down)
    ]
    row_sum = reduce_depth(grid, reduce_plane(grid, row_keep, row_send))

    d_attended = (
        matmul(d_attn_low, out_full, "tc,qc->tq")
        .astype(LOW)
        .reshape(tok_rows * HEADS, HEAD_DIM)
    )
    scores_again = attend_scores(queries, key_all, allowed)
    probs_again = jnp.exp(scores_again - log_total)
    d_values_all = matmul(probs_again.astype(LOW), d_attended, "qk,qd->kd")
    d_probs = matmul(d_attended, value_all, "qd,kd->qk")
    d_scores = probs_again * (d_probs - jnp.sum(d_probs * probs_again, axis=-1, keepdims=True))
    d_scores_low = d_scores.astype(LOW)
    d_keys_all = matmul(d_scores_low, queries, "qk,qd->kd") * HEAD_DIM ** (-0.5)
    d_kv_all = jnp.concatenate([d_keys_all, d_values_all], axis=1)
    near_back = shifted(d_kv_all[tok_rows : 2 * tok_rows].astype(LOW), -1)
    far_back = shifted(d_kv_all[:tok_rows].astype(LOW), -2)
    d_queries = matmul(d_scores_low, key_all, "qk,kd->qd") * HEAD_DIM ** (-0.5)
    d_q_proj, d_gain_query = query_pull(d_queries.reshape(tok_rows, HEADS, HEAD_DIM))
    d_kv = add_low(d_kv_all[2 * tok_rows :], near_back, far_back)
    d_k_proj, d_gain_key = key_pull(d_kv[:, :kd])
    d_proj = jnp.concatenate(
        [d_q_proj.astype(LOW), d_k_proj.astype(LOW), d_kv[:, kd:].astype(LOW)], axis=1
    )
    in_keep, in_send = halves(normed_low, half)
    grad_proj = [matmul(m, d_proj, "tc,tq->cq").astype(LOW) for m in (in_keep, in_send)]
    d_normed = matmul(d_proj, proj_full, "tq,cq->tc")
    d_tok_part, d_gain_in = in_pull(d_normed)
    tokens_grad = (d_residual + d_tok_part).astype(LOW)

    proj_keep, proj_send = [
        g.reshape(depth, half, side, side, proj_cols).transpose(0, 2, 3, 1, 4)
        for g in grad_proj
    ]
    proj_sum = reduce_depth(grid, reduce_plane(grid, proj_keep, proj_send))

    d_gains = [d_gain_in, d_gain_post, d_gain_pre, d_gain_ffn, d_gain_query, d_gain_key]
    d_all = jnp.concatenate([g.reshape(depth, -1) for g in d_gains], axis=1)
    lanes = 128
    pad = -(-gain_len // lanes) * lanes - gain_len
    d_all = jnp.pad(d_all, ((0, 0), (0, pad))).reshape(depth, -1, lanes)
    d_all = add_low(d_all, grid.over_core(d_all.astype(LOW)))
    low_all = d_all.astype(LOW)
    d_all = add_low(d_all, *[grid.over_first(low_all, k) for k in range(1, side)])
    low_all = d_all.astype(LOW)
    d_all = add_low(d_all, *[grid.over_second(low_all, k) for k in range(1, side)])
    gain_total = reduce_depth(grid, d_all.astype(LOW)).reshape(-1)
    gain_outs = [gain_total[s : s + n] for s, n in zip(gain_starts, gain_sizes)]

    def whole(block):
        return jnp.stack(gather_core(grid, gather_plane(grid, block.astype(LOW))))

    pair_out = whole(pair_sum).transpose(0, 3, 1, 2, 4).reshape(rows, spots, 2, ff_cols)
    pair_out = pair_out.astype(F32)
    total_gate = pair_out[:, :, 0].reshape(rows, ff)
    total_up = pair_out[:, :, 1].reshape(rows, ff)
    row_out = whole(row_sum).astype(F32)
    total_out = row_out[:, :, :, :out_part].reshape(out_rows, width)
    total_down = row_out[:, :, :, out_part:].reshape(down_rows, width)
    proj_out = whole(proj_sum).transpose(0, 3, 1, 2, 4).reshape(rows, qd + 2 * kd).astype(F32)
    return (
        block_out,
        tokens_grad,
        proj_out[:, :qd],
        proj_out[:, qd : qd + kd],
        proj_out[:, qd + kd :],
        total_out,
        total_gate,
        total_up,
        total_down,
        gain_outs[0],
        gain_outs[4],
        gain_outs[5],
        gain_outs[1],
        gain_outs[2],
        gain_outs[3],
    )


def solution(mesh):
    rows, cols, vec = P(ALL, None), P("shard", None), P("shard")
    return jax.shard_map(
        local,
        mesh=mesh,
        in_specs=(rows, rows, P()) + (cols,) * 7 + (vec,) * 6,
        out_specs=(rows, rows) + (cols,) * 7 + (vec,) * 6,
        check_vma=False,
    )
```

```python
import math

import jax
import jax.numpy as jnp
from jax import lax
from jax.experimental import pallas as pl
from jax.experimental.pallas import tpu as pltpu
from jax.sharding import PartitionSpec as P

HEADS = 4
HEAD_DIM = 256
WINDOW = 512
EPS = 1e-06
NEGATIVE = -1e30
ALL = ("rep", "shard")
LOW = jnp.bfloat16
F32 = jnp.float32


class Grid:
    def __init__(self):
        reps = lax.axis_size("rep")
        self.depth = lax.axis_size("shard")
        self.side = math.isqrt(reps // 2)
        assert 2 * self.side * self.side == reps
        rep = lax.axis_index("rep")
        self.z = lax.axis_index("shard")
        self.core = rep % 2
        col = (rep // 2) % self.side
        row = rep // (2 * self.side)
        self.first = jnp.where(self.core == 0, col, row)
        self.second = jnp.where(self.core == 0, row, col)
        self.place = self.second * self.side + self.first

    def pairs(self, move):
        side, depth = self.side, self.depth
        found = []
        for y in range(side):
            for x in range(side):
                for c in range(2):
                    for z in range(depth):
                        ty, tx, tc, tz = move(y, x, c, z)
                        source = ((y * side + x) * 2 + c) * depth + z
                        found.append((source, ((ty * side + tx) * 2 + tc) * depth + tz))
        return found

    def over_first(self, array, by):
        n = self.side
        return lax.ppermute(
            array,
            ALL,
            self.pairs(
                lambda y, x, c, z: (y, (x - by) % n, c, z) if c == 0 else ((y - by) % n, x, c, z)
            ),
        )

    def over_second(self, array, by):
        n = self.side
        return lax.ppermute(
            array,
            ALL,
            self.pairs(
                lambda y, x, c, z: ((y - by) % n, x, c, z) if c == 0 else (y, (x - by) % n, c, z)
            ),
        )

    def over_depth(self, array, by):
        return lax.ppermute(
            array, ALL, self.pairs(lambda y, x, c, z: (y, x, c, (z - by) % self.depth))
        )

    def over_core(self, array):
        return lax.ppermute(array, ALL, self.pairs(lambda y, x, c, z: (y, x, 1 - c, z)))


def in_order(parts, index):
    n = len(parts)
    if n == 1:
        return list(parts)
    if n == 2:
        own, other = parts
        return [jnp.where(index == 0, own, other), jnp.where(index == 0, other, own)]
    rolled = jnp.roll(jnp.stack(parts), index, axis=0)
    return [rolled[i] for i in range(n)]


def place_shards(parts, z):
    n = len(parts)
    branches = [
        (lambda *a, s=s: jnp.concatenate([a[(m - s) % n] for m in range(n)], axis=0))
        for s in range(n)
    ]
    return lax.switch(z, branches, *parts)


def gather_plane(grid, block):
    n = grid.side
    line = jnp.stack(
        in_order([block] + [grid.over_first(block, k) for k in range(1, n)], grid.first)
    )
    return jnp.stack(
        in_order([line] + [grid.over_second(line, k) for k in range(1, n)], grid.second)
    )


def gather_core(grid, half):
    return in_order([half, grid.over_core(half)], grid.core)


def take(array, index, axis):
    return lax.dynamic_index_in_dim(array, index, axis, keepdims=False)


def add_low(a, *others):
    total = a.astype(F32)
    for b in others:
        total = total + b.astype(F32)
    return total


def reduce_plane(grid, keep, send, extra=None):
    n = grid.side
    total = add_low(keep, grid.over_core(send)).astype(LOW)
    got = [
        grid.over_first(take(total, (grid.first - k) % n, 2), k) for k in range(1, n)
    ]
    total = add_low(take(total, grid.first, 2), *got).astype(LOW)
    got = [
        grid.over_second(take(total, (grid.second - k) % n, 1), k) for k in range(1, n)
    ]
    return add_low(take(total, grid.second, 1), *got).astype(LOW)


def reduce_depth(grid, total):
    n = grid.depth
    got = [grid.over_depth(take(total, (grid.z - k) % n, 0), k) for k in range(1, n)]
    return add_low(take(total, grid.z, 0), *got)


def shifted(array, by):
    peers = lax.axis_size(ALL)
    pairs = [(i, i + by) for i in range(peers) if 0 <= i + by < peers]
    return lax.ppermute(array, ALL, pairs)


def scaled(vector, scale_gain):
    inv_root = lax.rsqrt(jnp.mean(vector * vector, axis=-1, keepdims=True) + EPS)
    return vector * inv_root * (1.0 + scale_gain)


def places(glob_index, lengths):
    seq_ends = jnp.sum(
        jnp.where(
            jnp.arange(lengths.shape[0])[:, None] >= jnp.arange(lengths.shape[0])[None, :],
            lengths[None, :],
            0,
        ),
        axis=1,
    )
    before = seq_ends[None, :] <= glob_index[:, None]
    segment = jnp.sum(before.astype(jnp.int32), axis=1)
    seq_start = jnp.sum(jnp.where(before, lengths[None, :], 0), axis=1)
    return (segment, glob_index - seq_start)


def turning(position, width):
    half_width = width // 2
    frequency = jnp.exp(
        jnp.arange(half_width, dtype=F32) * (-2.0 * math.log(10000.0) / width)
    )
    angles = position.astype(F32)[:, None] * frequency[None, :]
    return (jnp.cos(angles), jnp.sin(angles))


def rotate(vector, cos_table, sin_table):
    half_width = vector.shape[-1] // 2
    first_half = vector[..., :half_width]
    second_half = vector[..., half_width:]
    return jnp.concatenate(
        [
            first_half * cos_table - second_half * sin_table,
            second_half * cos_table + first_half * sin_table,
        ],
        axis=-1,
    )


def geglu(gate_proj, up_proj):
    return jax.nn.gelu(gate_proj, approximate=True) * up_proj


def matmul(left, right, pattern):
    return jnp.einsum(pattern, left, right, preferred_element_type=F32)


def attend_scores(queries, key_all, allowed):
    scores = matmul(queries, key_all, "qd,kd->qk") * HEAD_DIM ** (-0.5)
    return jnp.where(allowed, scores, NEGATIVE)


def local_plain(
    tokens,
    cotangent,
    seq_lengths,
    w_query,
    w_key,
    w_value,
    w_out,
    w_gate,
    w_up,
    w_down,
    g_in,
    g_query,
    g_key,
    g_post,
    g_pre,
    g_ffn,
):
    grid = Grid()
    depth, side = grid.depth, grid.side
    spots = side * side
    tok_rows, width = tokens.shape
    rows = w_query.shape[0]
    half = rows // 2
    qd, kd = w_query.shape[1], w_key.shape[1]
    out_rows, down_rows, ff = w_out.shape[0], w_down.shape[0], w_gate.shape[1]
    proj_cols = (qd + 2 * kd) // spots
    ff_cols = ff // spots
    out_part, down_part = out_rows // (2 * spots), down_rows // (2 * spots)

    near_tok = shifted(tokens, 1)
    far_tok = shifted(tokens, 2)

    w_proj = jnp.concatenate([w_query, w_key, w_value], axis=1)
    gains_own = jnp.concatenate([g_in, g_post, g_pre, g_ffn, g_query, g_key])
    gain_len = gains_own.shape[0]
    proj_mine = lax.dynamic_slice(
        w_proj, (grid.core * half, grid.place * proj_cols), (half, proj_cols)
    )
    gain_rows = -(-gain_len // (proj_cols * 16)) * 16
    gain_block = jnp.pad(gains_own, (0, gain_rows * proj_cols - gain_len)).reshape(
        gain_rows, proj_cols
    )
    row_mine = jnp.concatenate(
        [
            lax.dynamic_slice_in_dim(
                w_out, (grid.core * spots + grid.place) * out_part, out_part, 0
            ),
            lax.dynamic_slice_in_dim(
                w_down, (grid.core * spots + grid.place) * down_part, down_part, 0
            ),
        ],
        axis=0,
    )
    pair_mine = jnp.concatenate(
        [
            lax.dynamic_slice(w, (grid.core * half, grid.place * ff_cols), (half, ff_cols))
            for w in (w_gate, w_up)
        ],
        axis=1,
    )

    proj_sent = jnp.concatenate([proj_mine, gain_block], axis=0)
    proj_got = [grid.over_depth(proj_sent, k) for k in range(1, depth)]
    row_got = [grid.over_depth(row_mine, k) for k in range(1, depth)]
    pair_got = [grid.over_depth(pair_mine, k) for k in range(1, depth)]

    gains_all = place_shards(
        [gain_block[None]] + [g[None, half:] for g in proj_got], grid.z
    ).reshape(depth, -1)[:, :gain_len].astype(F32)
    gain_sizes = [g.shape[0] for g in (g_in, g_post, g_pre, g_ffn, g_query, g_key)]
    gain_starts = [sum(gain_sizes[:i]) for i in range(len(gain_sizes))]
    gain_in, gain_post, gain_pre, gain_ffn, gain_query, gain_key = [
        gains_all[:, s : s + n].reshape(-1) for s, n in zip(gain_starts, gain_sizes)
    ]

    proj_halves = gather_core(
        grid, gather_plane(grid, jnp.stack([g[:half] for g in proj_got]))
    )
    proj_parts = jnp.stack(proj_halves).transpose(3, 0, 4, 1, 2, 5)
    proj_parts = proj_parts.reshape(depth - 1, rows, qd + 2 * kd)
    proj_full = place_shards(
        [w_proj[None]] + [proj_parts[k : k + 1] for k in range(depth - 1)], grid.z
    ).reshape(depth * rows, qd + 2 * kd)

    row_halves = jnp.stack(gather_core(grid, gather_plane(grid, jnp.stack(row_got))))
    row_halves = row_halves.transpose(3, 0, 1, 2, 4, 5).reshape(
        depth - 1, 2, spots, out_part + down_part, width
    )
    out_parts = row_halves[:, :, :, :out_part].reshape(depth - 1, out_rows, width)
    down_parts = row_halves[:, :, :, out_part:].reshape(depth - 1, down_rows, width)
    out_full = place_shards(
        [w_out[None]] + [out_parts[k : k + 1] for k in range(depth - 1)], grid.z
    ).reshape(depth * out_rows, width)
    down_full = place_shards(
        [w_down[None]] + [down_parts[k : k + 1] for k in range(depth - 1)], grid.z
    ).reshape(depth * down_rows, width)

    pair_own = jnp.stack(
        [w_gate.reshape(rows, spots, ff_cols), w_up.reshape(rows, spots, ff_cols)], axis=2
    ).reshape(rows, 2 * ff)
    pair_parts = jnp.stack(gather_core(grid, gather_plane(grid, jnp.stack(pair_got))))
    pair_parts = pair_parts.transpose(3, 0, 4, 1, 2, 5).reshape(depth - 1, rows, 2 * ff)
    pair_full = place_shards(
        [pair_own[None]] + [pair_parts[k : k + 1] for k in range(depth - 1)], grid.z
    ).reshape(depth * rows, 2 * ff)

    device = lax.axis_index(ALL)
    glob_index = device * tok_rows + jnp.arange(-2 * tok_rows, tok_rows, dtype=jnp.int32)
    segment, position = places(glob_index, seq_lengths)
    own_glob = glob_index[2 * tok_rows :]
    own_seg = segment[2 * tok_rows :]
    cos_all, sin_all = turning(position, HEAD_DIM)
    cos_table, sin_table = cos_all[2 * tok_rows :], sin_all[2 * tok_rows :]
    allowed = (
        (segment[None, :] == own_seg[:, None])
        & (glob_index[None, :] <= own_glob[:, None])
        & (own_glob[:, None] - glob_index[None, :] < WINDOW)
        & (glob_index[None, :] >= 0)
    )
    allowed = jnp.repeat(allowed, HEADS, axis=0)

    def query_side(q_proj, scale_gain):
        return rotate(
            scaled(q_proj.reshape(tok_rows, HEADS, HEAD_DIM), scale_gain),
            cos_table[:, None, :],
            sin_table[:, None, :],
        )

    def key_side(k_proj, scale_gain):
        return rotate(scaled(k_proj, scale_gain), cos_table, sin_table)

    tok_float = tokens.astype(F32)
    normed, in_pull = jax.vjp(scaled, tok_float, gain_in)
    normed_low = normed.astype(LOW)
    halo = jnp.concatenate([far_tok, near_tok], axis=0).astype(F32)
    halo_low = scaled(halo, gain_in).astype(LOW)
    proj_own = matmul(normed_low, proj_full, "tc,cq->tq")
    q_proj = proj_own[:, :qd]
    k_proj = proj_own[:, qd : qd + kd]
    v_proj = proj_own[:, qd + kd :]
    halo_proj = matmul(halo_low, proj_full[:, qd:], "tc,cq->tq")
    halo_keys = rotate(
        scaled(halo_proj[:, :kd], gain_key), cos_all[: 2 * tok_rows], sin_all[: 2 * tok_rows]
    )
    query_val, query_pull = jax.vjp(query_side, q_proj, gain_query)
    queries = query_val.astype(LOW).reshape(tok_rows * HEADS, HEAD_DIM)
    key_val, key_pull = jax.vjp(key_side, k_proj, gain_key)
    key_all = jnp.concatenate([halo_keys, key_val], axis=0).astype(LOW)
    value_all = jnp.concatenate([halo_proj[:, kd:], v_proj], axis=0).astype(LOW)
    scores = attend_scores(queries, key_all, allowed)
    row_max = jnp.max(scores, axis=-1, keepdims=True)
    exponent = jnp.exp(scores - row_max)
    row_total = jnp.sum(exponent, axis=-1, keepdims=True)
    attn_probs = exponent / row_total
    log_total = row_max + jnp.log(row_total)
    attended = matmul(attn_probs.astype(LOW), value_all, "qk,kd->qd")
    attended_low = attended.reshape(tok_rows, HEADS * HEAD_DIM).astype(LOW)
    attn_proj = matmul(attended_low, out_full, "tq,qc->tc")
    post_val, post_pull = jax.vjp(scaled, attn_proj, gain_post)
    residual = tok_float + post_val
    pre_val, pre_pull = jax.vjp(scaled, residual, gain_pre)
    normed_two = pre_val.astype(LOW)
    both = matmul(normed_two, pair_full, "tc,cf->tf").reshape(tok_rows, spots, 2, ff_cols)
    gate_proj, up_proj = both[:, :, 0], both[:, :, 1]
    mixed_val, mixed_pull = jax.vjp(geglu, gate_proj, up_proj)
    mixed_low = mixed_val.astype(LOW).reshape(tok_rows, ff)
    ffn_proj = matmul(mixed_low, down_full, "tf,fc->tc")
    ffn_val, ffn_pull = jax.vjp(scaled, ffn_proj, gain_ffn)
    block_out = (residual + ffn_val).astype(LOW)

    def halves(array, part):
        split = array.reshape(tok_rows, depth, 2, part)
        keep = take(split, grid.core, 2).reshape(tok_rows, depth * part)
        send = take(split, 1 - grid.core, 2).reshape(tok_rows, depth * part)
        return keep, send

    upstream = cotangent.astype(F32)
    d_ffn_proj, d_gain_ffn = ffn_pull(upstream)
    d_ffn_low = d_ffn_proj.astype(LOW)
    mixed_keep, mixed_send = halves(mixed_low, down_part * spots)
    grad_down = [matmul(m, d_ffn_low, "tf,tc->fc").astype(LOW) for m in (mixed_keep, mixed_send)]
    d_mixed = matmul(d_ffn_low, down_full, "tc,fc->tf").reshape(tok_rows, spots, ff_cols)
    d_gate, d_up = mixed_pull(d_mixed)
    d_both = jnp.stack([d_gate.astype(LOW), d_up.astype(LOW)], axis=2).reshape(tok_rows, 2 * ff)
    two_keep, two_send = halves(normed_two, half)
    grad_pair = [matmul(m, d_both, "tc,tf->cf").astype(LOW) for m in (two_keep, two_send)]
    d_normed_two = matmul(d_both, pair_full, "tf,cf->tc")
    d_resid_part, d_gain_pre = pre_pull(d_normed_two)
    d_residual = upstream + d_resid_part
    d_attn_proj, d_gain_post = post_pull(d_residual)
    d_attn_low = d_attn_proj.astype(LOW)
    att_keep, att_send = halves(attended_low, out_part * spots)
    grad_out = [matmul(m, d_attn_low, "tq,tc->qc").astype(LOW) for m in (att_keep, att_send)]

    pair_keep, pair_send = [
        g.reshape(depth, half, side, side, 2 * ff_cols).transpose(0, 2, 3, 1, 4)
        for g in grad_pair
    ]
    pair_sum = reduce_depth(grid, reduce_plane(grid, pair_keep, pair_send))
    row_keep, row_send = [
        jnp.concatenate(
            [
                o.reshape(depth, side, side, out_part, width),
                d.reshape(depth, side, side, down_part, width),
            ],
            axis=3,
        )
        for o, d in zip(grad_out, grad_down)
    ]
    row_sum = reduce_depth(grid, reduce_plane(grid, row_keep, row_send))

    d_attended = (
        matmul(d_attn_low, out_full, "tc,qc->tq")
        .astype(LOW)
        .reshape(tok_rows * HEADS, HEAD_DIM)
    )
    scores_again = attend_scores(queries, key_all, allowed)
    probs_again = jnp.exp(scores_again - log_total)
    d_values_all = matmul(probs_again.astype(LOW), d_attended, "qk,qd->kd")
    d_probs = matmul(d_attended, value_all, "qd,kd->qk")
    d_scores = probs_again * (d_probs - jnp.sum(d_probs * probs_again, axis=-1, keepdims=True))
    d_scores_low = d_scores.astype(LOW)
    d_keys_all = matmul(d_scores_low, queries, "qk,qd->kd") * HEAD_DIM ** (-0.5)
    d_kv_all = jnp.concatenate([d_keys_all, d_values_all], axis=1)
    near_back = shifted(d_kv_all[tok_rows : 2 * tok_rows].astype(LOW), -1)
    far_back = shifted(d_kv_all[:tok_rows].astype(LOW), -2)
    d_queries = matmul(d_scores_low, key_all, "qk,kd->qd") * HEAD_DIM ** (-0.5)
    d_q_proj, d_gain_query = query_pull(d_queries.reshape(tok_rows, HEADS, HEAD_DIM))
    d_kv = add_low(d_kv_all[2 * tok_rows :], near_back, far_back)
    d_k_proj, d_gain_key = key_pull(d_kv[:, :kd])
    d_proj = jnp.concatenate(
        [d_q_proj.astype(LOW), d_k_proj.astype(LOW), d_kv[:, kd:].astype(LOW)], axis=1
    )
    in_keep, in_send = halves(normed_low, half)
    grad_proj = [matmul(m, d_proj, "tc,tq->cq").astype(LOW) for m in (in_keep, in_send)]
    d_normed = matmul(d_proj, proj_full, "tq,cq->tc")
    d_tok_part, d_gain_in = in_pull(d_normed)
    tokens_grad = (d_residual + d_tok_part).astype(LOW)

    proj_keep, proj_send = [
        g.reshape(depth, half, side, side, proj_cols).transpose(0, 2, 3, 1, 4)
        for g in grad_proj
    ]
    proj_sum = reduce_depth(grid, reduce_plane(grid, proj_keep, proj_send))

    d_gains = [d_gain_in, d_gain_post, d_gain_pre, d_gain_ffn, d_gain_query, d_gain_key]
    d_all = jnp.concatenate([g.reshape(depth, -1) for g in d_gains], axis=1)
    lanes = 128
    pad = -(-gain_len // lanes) * lanes - gain_len
    d_all = jnp.pad(d_all, ((0, 0), (0, pad))).reshape(depth, -1, lanes)
    d_all = add_low(d_all, grid.over_core(d_all.astype(LOW)))
    low_all = d_all.astype(LOW)
    d_all = add_low(d_all, *[grid.over_first(low_all, k) for k in range(1, side)])
    low_all = d_all.astype(LOW)
    d_all = add_low(d_all, *[grid.over_second(low_all, k) for k in range(1, side)])
    gain_total = reduce_depth(grid, d_all.astype(LOW)).reshape(-1)
    gain_outs = [gain_total[s : s + n] for s, n in zip(gain_starts, gain_sizes)]

    def whole(block):
        return jnp.stack(gather_core(grid, gather_plane(grid, block.astype(LOW))))

    pair_out = whole(pair_sum).transpose(0, 3, 1, 2, 4).reshape(rows, spots, 2, ff_cols)
    pair_out = pair_out.astype(F32)
    total_gate = pair_out[:, :, 0].reshape(rows, ff)
    total_up = pair_out[:, :, 1].reshape(rows, ff)
    row_out = whole(row_sum).astype(F32)
    total_out = row_out[:, :, :, :out_part].reshape(out_rows, width)
    total_down = row_out[:, :, :, out_part:].reshape(down_rows, width)
    proj_out = whole(proj_sum).transpose(0, 3, 1, 2, 4).reshape(rows, qd + 2 * kd).astype(F32)
    return (
        block_out,
        tokens_grad,
        proj_out[:, :qd],
        proj_out[:, qd : qd + kd],
        proj_out[:, qd + kd :],
        total_out,
        total_gate,
        total_up,
        total_down,
        gain_outs[0],
        gain_outs[4],
        gain_outs[5],
        gain_outs[1],
        gain_outs[2],
        gain_outs[3],
    )


STEPS = ((0, 0), (1, 0), (0, 1), (1, 1))
NT = (((1,), (1,)), ((), ()))
TN = (((0,), (0,)), ((), ()))
NN = (((1,), (0,)), ((), ()))
GELU_A = math.sqrt(2.0 / math.pi)
GELU_B = 0.044715


def dot(left, right, dims=NN):
    return lax.dot_general(left, right, dims, preferred_element_type=F32)


def spot_of(co, core_side, step):
    core, first, second = co[1], co[2], co[3]
    if core_side == 0:
        half, b1, b2 = core, first, second
    else:
        half, b1, b2 = 1 - core, second, first
    b1 = lax.rem(b1 + step[0], 2)
    b2 = lax.rem(b2 + step[1], 2)
    return half, 2 * b2 + b1


def each_piece(co, refs):
    for side in range(2):
        for i, step in enumerate(STEPS):
            half, place = spot_of(co, side, step)
            yield refs[4 * side + i], half, place


def at_rows(start, size, tile=16):
    return pl.ds(pl.multiple_of(start, tile), size)


def run_all(copies):
    for copy in copies:
        copy.start()


def wait_all(copies):
    for copy in copies:
        copy.wait()


def root_of(v):
    return lax.rsqrt(jnp.mean(v * v, axis=-1, keepdims=True) + EPS)


def norm_back(v, root, gain_one, dy):
    u = dy * gain_one
    dv = root * u - v * (root * root * root) * jnp.mean(u * v, axis=-1, keepdims=True)
    return dv, jnp.sum(dy * v * root, axis=0, keepdims=True)


def turn(v, cos, sin):
    h = v.shape[-1] // 2
    a, b = v[:, :h], v[:, h:]
    return jnp.concatenate([a * cos - b * sin, b * cos + a * sin], axis=-1)


def turn_back(v, cos, sin):
    h = v.shape[-1] // 2
    a, b = v[:, :h], v[:, h:]
    return jnp.concatenate([a * cos + b * sin, b * cos - a * sin], axis=-1)


VM = pl.BlockSpec(memory_space=pltpu.VMEM)
SM = pl.BlockSpec(memory_space=pltpu.SMEM)
AN = pl.BlockSpec(memory_space=pl.ANY)


def call(kernel, outs, ins, args, scratch, name, flops, moved):
    return pl.pallas_call(
        kernel,
        out_shape=[jax.ShapeDtypeStruct(s, d) for s, d, _ in outs],
        in_specs=ins,
        out_specs=[m for _, _, m in outs],
        scratch_shapes=scratch,
        cost_estimate=pl.CostEstimate(flops=flops, bytes_accessed=moved, transcendentals=0),
        compiler_params=pltpu.CompilerParams(vmem_limit_bytes=60 * 1024 * 1024),
        name=name,
    )(*args)


def pack_kernel(co, w_proj, w_out, w_down, w_gate, w_up, gains, proj_o, row_o, pair_o, sem):
    core, place = co[1], 2 * co[3] + co[2]
    half, cols = w_proj.shape[0] // 2, proj_o.shape[1]
    ff_cols = pair_o.shape[1] // 2
    out_part = w_out.shape[0] // 8
    down_part = w_down.shape[0] // 8
    rows = at_rows(core * half, half)
    spot = core * 4 + place
    copies = [
        (w_proj.at[rows, at_rows(place * cols, cols, 128)], proj_o.at[pl.ds(0, half)]),
        (w_out.at[at_rows(spot * out_part, out_part)], row_o.at[pl.ds(0, out_part)]),
        (w_down.at[at_rows(spot * down_part, down_part)], row_o.at[pl.ds(out_part, down_part)]),
        (
            w_gate.at[rows, at_rows(place * ff_cols, ff_cols, 128)],
            pair_o.at[:, pl.ds(0, ff_cols)],
        ),
        (
            w_up.at[rows, at_rows(place * ff_cols, ff_cols, 128)],
            pair_o.at[:, pl.ds(ff_cols, ff_cols)],
        ),
    ]
    copies = [pltpu.make_async_copy(s, d, sem.at[i]) for i, (s, d) in enumerate(copies)]
    run_all(copies)
    proj_o[half:, :] = gains[...]
    wait_all(copies)


def attend_kernel(co, tok, near, far, gains, cos, sin, bias, w_query, w_key, w_value, *rest):
    pieces = rest[:8]
    normed_o, proj_o, queries_o, keys_o, values_o, attended_o, lse_o, w_o, sem = rest[8:]
    z = co[0]
    n = tok.shape[0]
    rows, qd = w_query.shape
    kd = w_key.shape[1]
    half = rows // 2
    cols = pieces[0].shape[2]
    own = at_rows(z * rows, rows)
    copies = [
        (w_query, w_o.at[own, pl.ds(0, qd)]),
        (w_key, w_o.at[own, pl.ds(qd, kd)]),
        (w_value, w_o.at[own, pl.ds(qd + kd, kd)]),
    ]
    for ref, side, place in each_piece(co, pieces):
        for k in range(3):
            shard = lax.rem(z + k + 1, 4)
            copies.append(
                (
                    ref.at[k],
                    w_o.at[
                        at_rows(shard * rows + side * half, half),
                        at_rows(place * cols, cols, 128),
                    ],
                )
            )
    copies = [pltpu.make_async_copy(s, d, sem) for s, d in copies]
    run_all(copies)
    gain_in = 1.0 + gains[0:1, :]
    gain_query = 1.0 + gains[4:5, :HEAD_DIM]
    gain_key = 1.0 + gains[5:6, :HEAD_DIM]

    def normed_of(ref):
        v = ref[...].astype(F32)
        return (v * root_of(v) * gain_in).astype(LOW)

    low = normed_of(tok)
    normed_o[...] = low
    halo = [normed_of(far), normed_of(near)]
    wait_all(copies)
    proj = dot(low, w_o[...])
    proj_o[...] = proj[:, : qd + kd]
    for i in range(3):
        kv = proj[:, qd:] if i == 2 else dot(halo[i], w_o[:, qd:])
        at = slice(i * n, (i + 1) * n)
        k = kv[:, :kd]
        k = turn(k * root_of(k) * gain_key, cos[at, :], sin[at, :])
        keys_o[at, :] = k.astype(LOW)
        values_o[at, :] = kv[:, kd:].astype(LOW)
    own_cos, own_sin = cos[2 * n :, :], sin[2 * n :, :]
    for h in range(HEADS):
        at = slice(h * HEAD_DIM, (h + 1) * HEAD_DIM)
        q = proj[:, at]
        q = turn(q * root_of(q) * gain_query, own_cos, own_sin).astype(LOW)
        queries_o[:, at] = q
        scores = dot(q, keys_o[...], NT) * HEAD_DIM ** (-0.5) + bias[...]
        top = jnp.max(scores, axis=-1, keepdims=True)
        e = jnp.exp(scores - top)
        total = jnp.sum(e, axis=-1, keepdims=True)
        p = e / total
        lse_o[h] = jnp.broadcast_to(top + jnp.log(total), lse_o.shape[1:])
        attended_o[:, at] = dot(p.astype(LOW), values_o[...]).astype(LOW)


def out_copies(co, grad, row_of, size, cols_of, refs, sem, dst_rows=None):
    z = co[0]
    found = []
    for side in range(2):
        late, mid, last = refs[3 * side : 3 * side + 3]
        for step in STEPS:
            half, place = spot_of(co, side, step)
            for k in range(4):
                shard = lax.rem(z + k, 4)
                target = late.at[step[1], k] if step[0] else (mid if step[1] else last).at[k]
                if dst_rows is not None:
                    target = target.at[dst_rows]
                source = grad
                if row_of is not None:
                    source = grad.at[at_rows(row_of(shard, half, place), size)]
                    if cols_of is not None:
                        width = cols_of
                        source = grad.at[
                            at_rows(row_of(shard, half, place), size),
                            at_rows(place * width, width, 128),
                        ]
                found.append(pltpu.make_async_copy(source, target, sem))
    return found


def ffn_kernel(co, tok, cot, att, gains, w_out, w_down, w_gate, w_up, *rest):
    row_pieces, pair_pieces = rest[:8], rest[8:16]
    block_o, resid_o, d_att_o, gain_o = rest[16:20]
    pair_refs, row_refs = rest[20:26], rest[26:32]
    (
        out_w,
        down_w,
        pair_w,
        out_g,
        down_g,
        pair_g,
        two_s,
        act_s,
        back_s,
        mixed_s,
        sems,
    ) = rest[32:]
    z = co[0]
    out_rows, down_rows = w_out.shape[0], w_down.shape[0]
    rows, ff = w_gate.shape
    half = rows // 2
    fc = ff // 4
    out_part, down_part = out_rows // 8, down_rows // 8

    def copies_of(pairs, sem):
        return [pltpu.make_async_copy(s, d, sem) for s, d in pairs]

    into_out = [(w_out, out_w.at[at_rows(z * out_rows, out_rows)])]
    into_down = [(w_down, down_w.at[at_rows(z * down_rows, down_rows)])]
    for ref, side, place in each_piece(co, row_pieces):
        for k in range(3):
            shard = lax.rem(z + k + 1, 4)
            spot = side * 4 + place
            into_out.append(
                (
                    ref.at[k, pl.ds(0, out_part)],
                    out_w.at[at_rows(shard * out_rows + spot * out_part, out_part)],
                )
            )
            into_down.append(
                (
                    ref.at[k, pl.ds(out_part, down_part)],
                    down_w.at[at_rows(shard * down_rows + spot * down_part, down_part)],
                )
            )
    into_pair = []
    for q in range(4):
        for i, w in enumerate((w_gate, w_up)):
            into_pair.append(
                (
                    w.at[:, pl.ds(q * fc, fc)],
                    pair_w.at[at_rows(z * rows, rows), pl.ds((2 * q + i) * fc, fc)],
                )
            )
    for ref, side, place in each_piece(co, pair_pieces):
        for k in range(3):
            shard = lax.rem(z + k + 1, 4)
            into_pair.append(
                (
                    ref.at[k],
                    pair_w.at[
                        at_rows(shard * rows + side * half, half),
                        at_rows(place * 2 * fc, 2 * fc, 128),
                    ],
                )
            )
    into_out = copies_of(into_out, sems.at[0])
    into_pair = copies_of(into_pair, sems.at[1])
    into_down = copies_of(into_down, sems.at[2])
    run_all(into_out)
    run_all(into_pair)
    run_all(into_down)

    gain_post = 1.0 + gains[1:2, :]
    gain_pre = 1.0 + gains[2:3, :]
    gain_ffn = 1.0 + gains[3:4, :]
    wait_all(into_out)
    attn = dot(att[...], out_w[...])
    attn_root = root_of(attn)
    residual = tok[...].astype(F32) + attn * attn_root * gain_post
    res_root = root_of(residual)
    two_s[...] = (residual * res_root * gain_pre).astype(LOW)
    wait_all(into_pair)
    wait_all(into_down)
    ffn = None
    for q in range(4):
        both = dot(two_s[...], pair_w[:, 2 * q * fc : 2 * (q + 1) * fc])
        gate, up = both[:, :fc], both[:, fc:]
        t = jnp.tanh(GELU_A * (gate + GELU_B * gate * gate * gate))
        act = 0.5 * gate * (1.0 + t)
        slope = 0.5 * (1.0 + t) + 0.5 * gate * (1.0 - t * t) * (
            GELU_A * (1.0 + 3.0 * GELU_B * gate * gate)
        )
        at = slice(q * fc, (q + 1) * fc)
        act_s[:, at] = act
        back_s[:, at] = up * slope
        mixed = (act * up).astype(LOW)
        mixed_s[:, at] = mixed
        part = dot(mixed, down_w[at, :])
        ffn = part if ffn is None else ffn + part
    ffn_root = root_of(ffn)
    block_o[...] = (residual + ffn * ffn_root * gain_ffn).astype(LOW)

    upstream = cot[...].astype(F32)
    d_ffn, d_gain_ffn = norm_back(ffn, ffn_root, gain_ffn, upstream)
    d_ffn = d_ffn.astype(LOW)
    d_two = None
    for q in range(4):
        at = slice(q * fc, (q + 1) * fc)
        d_mixed = dot(d_ffn, down_w[at, :], NT)
        down_g[at, :] = dot(mixed_s[:, at], d_ffn, TN).astype(LOW)
        d_both = jnp.concatenate(
            [d_mixed * back_s[:, at], d_mixed * act_s[:, at]], axis=1
        ).astype(LOW)
        wide = slice(2 * q * fc, 2 * (q + 1) * fc)
        pair_g[:, wide] = dot(two_s[...], d_both, TN).astype(LOW)
        part = dot(d_both, pair_w[:, wide], NT)
        d_two = part if d_two is None else d_two + part
    pair_copies = out_copies(
        co,
        pair_g,
        lambda shard, side, place: shard * rows + side * half,
        half,
        2 * fc,
        pair_refs,
        sems.at[3],
    )
    down_copies = out_copies(
        co,
        down_g,
        lambda shard, side, place: shard * down_rows + (side * 4 + place) * down_part,
        down_part,
        None,
        row_refs,
        sems.at[4],
        pl.ds(out_part, down_part),
    )
    run_all(pair_copies)
    run_all(down_copies)
    d_res, d_gain_pre = norm_back(residual, res_root, gain_pre, d_two)
    d_res = upstream + d_res
    resid_o[...] = d_res
    d_attn, d_gain_post = norm_back(attn, attn_root, gain_post, d_res)
    d_attn = d_attn.astype(LOW)
    out_g[...] = dot(att[...], d_attn, TN).astype(LOW)
    outer_copies = out_copies(
        co,
        out_g,
        lambda shard, side, place: shard * out_rows + (side * 4 + place) * out_part,
        out_part,
        None,
        row_refs,
        sems.at[5],
        pl.ds(0, out_part),
    )
    run_all(outer_copies)
    d_att_o[...] = dot(d_attn, out_w[...], NT).astype(LOW)
    gain_o[0:1, :] = d_gain_post
    gain_o[1:2, :] = d_gain_pre
    gain_o[2:3, :] = d_gain_ffn
    gain_o[3:, :] = jnp.zeros_like(gain_o[3:, :])
    wait_all(pair_copies)
    wait_all(down_copies)
    wait_all(outer_copies)


def attend_back_kernel(
    queries, keys, values, d_att, lse, bias, proj, cos, sin, gains,
    d_query_o, near_o, far_o, own_o, gain_o, d_keys, d_values,
):
    n = queries.shape[0]
    kd = keys.shape[1]
    unit = HEAD_DIM ** (-0.5)
    gain_query = 1.0 + gains[4:5, :HEAD_DIM]
    own_cos, own_sin = cos[2 * n :, :], sin[2 * n :, :]
    gain_sum = None
    for h in range(HEADS):
        at = slice(h * HEAD_DIM, (h + 1) * HEAD_DIM)
        q, da = queries[:, at], d_att[:, at]
        scores = dot(q, keys[...], NT) * unit + bias[...]
        p = jnp.exp(scores - lse[h][:, :1])
        d_p = dot(da, values[...], NT)
        d_s = (p * (d_p - jnp.sum(d_p * p, axis=-1, keepdims=True))).astype(LOW)
        d_v = dot(p.astype(LOW), da, TN)
        d_k = dot(d_s, q, TN)
        if h == 0:
            d_values[...] = d_v
            d_keys[...] = d_k
        else:
            d_values[...] += d_v
            d_keys[...] += d_k
        d_q = turn_back(dot(d_s, keys[...]) * unit, own_cos, own_sin)
        v = proj[:, at]
        d_v_q, d_gain = norm_back(v, root_of(v), gain_query, d_q)
        d_query_o[:, at] = d_v_q.astype(LOW)
        gain_sum = d_gain if gain_sum is None else gain_sum + d_gain
    gain_o[...] = jnp.broadcast_to(gain_sum, gain_o.shape)
    for ref, start in ((far_o, 0), (near_o, n), (own_o, 2 * n)):
        ref[:, :kd] = (d_keys[start : start + n, :] * unit).astype(ref.dtype)
        ref[:, kd:] = d_values[start : start + n, :].astype(ref.dtype)


def proj_back_kernel(
    co, own, near, far, proj, cos, sin, gains, d_query, normed, tok, d_res, w, ffn_gains, q_gain,
    tokens_o, *rest,
):
    refs, (grad, low_tail, tail, sems) = rest[:6], rest[6:]
    n = tok.shape[0]
    qd = d_query.shape[1]
    kd = HEAD_DIM
    rows = w.shape[0] // 4
    half = rows // 2
    cols = w.shape[1] // 4
    width = tok.shape[1]
    d_kv = own[...] + near[...].astype(F32) + far[...].astype(F32)
    gain_key = 1.0 + gains[5:6, :kd]
    gain_in = 1.0 + gains[0:1, :]
    v = proj[:, qd : qd + kd]
    d_k = turn_back(d_kv[:, :kd], cos[2 * n :, :], sin[2 * n :, :])
    d_k, d_gain_key = norm_back(v, root_of(v), gain_key, d_k)
    d_proj = jnp.concatenate(
        [d_query[...], d_k.astype(LOW), d_kv[:, kd:].astype(LOW)], axis=1
    )
    grad[...] = dot(normed[...], d_proj, TN).astype(LOW)
    copies = out_copies(
        co,
        grad,
        lambda shard, side, place: shard * rows + side * half,
        half,
        cols,
        refs,
        sems.at[0],
        pl.ds(0, half),
    )
    run_all(copies)
    d_normed = dot(d_proj, w[...], NT)
    x = tok[...].astype(F32)
    d_x, d_gain_in = norm_back(x, root_of(x), gain_in, d_normed)
    tokens_o[...] = (d_res[...] + d_x).astype(LOW)
    tail[...] = jnp.zeros_like(tail)
    parts = [d_gain_in, ffn_gains[0:1, :], ffn_gains[1:2, :], ffn_gains[2:3, :]]
    for i, part in enumerate(parts):
        tail[2 * i : 2 * i + 1, :] = part[:, :cols]
        tail[2 * i + 1 : 2 * i + 2, : width - cols] = part[:, cols:]
    tail[8:9, :kd] = q_gain[0:1, :]
    tail[9:10, :kd] = d_gain_key
    low_tail[...] = tail[...].astype(LOW)
    tail_rows = low_tail.shape[0]
    more = out_copies(
        co, low_tail, None, None, None, refs, sems.at[1], pl.ds(half, tail_rows)
    )
    run_all(more)
    wait_all(copies)
    wait_all(more)


def unpack_pair_kernel(co, *rest):
    pieces, (gate_o, up_o) = rest[:8], rest[8:]
    half = gate_o.shape[0] // 2
    fc = gate_o.shape[1] // 4
    for ref, side, place in each_piece(co, pieces):
        at = (at_rows(side * half, half), at_rows(place * fc, fc, 128))
        gate_o[at] = ref[:, :fc].astype(F32)
        up_o[at] = ref[:, fc:].astype(F32)


def unpack_row_kernel(co, *rest):
    pieces, (out_o, down_o) = rest[:8], rest[8:]
    out_part, down_part = out_o.shape[0] // 8, down_o.shape[0] // 8
    for ref, side, place in each_piece(co, pieces):
        spot = side * 4 + place
        out_o[at_rows(spot * out_part, out_part), :] = ref[:out_part, :].astype(F32)
        down_o[at_rows(spot * down_part, down_part), :] = ref[out_part:, :].astype(F32)


def unpack_proj_kernel(co, *rest):
    pieces, (query_o, key_o, value_o, tail_o, full) = rest[:8], rest[8:]
    half = query_o.shape[0] // 2
    cols = full.shape[1] // 4
    qd, kd = query_o.shape[1], key_o.shape[1]
    for ref, side, place in each_piece(co, pieces):
        full[at_rows(side * half, half), at_rows(place * cols, cols, 128)] = ref[
            :half, :
        ].astype(F32)
    query_o[...] = full[:, :qd]
    key_o[...] = full[:, qd : qd + kd]
    value_o[...] = full[:, qd + kd :]
    tail_o[...] = pieces[0][half:, :].astype(F32)


def spread(grid, block):
    side = grid.over_first(block, 1)
    own = [block, side, grid.over_second(block, 1), grid.over_second(side, 1)]
    return own + [grid.over_core(b) for b in own]


def ring(grid, block):
    found = [block]
    for _ in range(grid.depth - 1):
        found.append(grid.over_depth(found[-1], 1))
    return found[1:]


def gathered_sum(grid, arrays):
    keep_late, keep_mid, keep_last, send_late, send_mid, send_last = arrays
    late = add_low(keep_late, grid.over_core(send_late)).astype(LOW)
    mid_got, last_got = grid.over_core(send_mid), grid.over_core(send_last)
    late_got = grid.over_first(late, 1)
    mid = add_low(keep_mid, mid_got, late_got[1]).astype(LOW)
    second_got = grid.over_second(mid, 1)
    sums = [
        add_low(keep_last[k], last_got[k], late_got[0, k], second_got[k])
        for k in range(grid.depth)
    ]
    got = [grid.over_depth(sums[k].astype(LOW), -k) for k in range(1, grid.depth)]
    return add_low(sums[0], *got).astype(LOW)


def local_fast(
    tokens,
    cotangent,
    seq_lengths,
    w_query,
    w_key,
    w_value,
    w_out,
    w_gate,
    w_up,
    w_down,
    g_in,
    g_query,
    g_key,
    g_post,
    g_pre,
    g_ffn,
):
    grid = Grid()
    n, width = tokens.shape
    rows, qd = w_query.shape
    kd = w_key.shape[1]
    half = rows // 2
    out_rows, down_rows, ff = w_out.shape[0], w_down.shape[0], w_gate.shape[1]
    total_cols = qd + 2 * kd
    cols, fc = total_cols // 4, ff // 4
    out_part, down_part = out_rows // 8, down_rows // 8
    row_part = out_part + down_part
    coords = jnp.stack([grid.z, grid.core, grid.first, grid.second]).astype(jnp.int32)
    dma = pltpu.SemaphoreType.DMA

    w_proj = jnp.concatenate([w_query, w_key, w_value], axis=1)
    gains_own = jnp.concatenate([g_in, g_post, g_pre, g_ffn, g_query, g_key])
    gain_len = gains_own.shape[0]
    gain_block = jnp.pad(gains_own, (0, 16 * cols - gain_len)).reshape(16, cols)
    proj_mine, row_mine, pair_mine = call(
        pack_kernel,
        [
            ((half + 16, cols), LOW, VM),
            ((row_part, width), LOW, VM),
            ((half, 2 * fc), LOW, VM),
        ],
        [SM] + [AN] * 5 + [VM],
        (coords, w_proj, w_out, w_down, w_gate, w_up, gain_block),
        [dma((5,))],
        "pack",
        0,
        2_000_000,
    )
    proj_got = ring(grid, proj_mine)
    near_tok = shifted(tokens, 1)
    far_tok = shifted(tokens, 2)
    row_got = ring(grid, row_mine)
    pair_got = ring(grid, pair_mine)
    proj_pieces = spread(grid, jnp.stack([g[:half] for g in proj_got]))
    row_pieces = spread(grid, jnp.stack(row_got))
    pair_pieces = spread(grid, jnp.stack(pair_got))

    rel = jnp.stack([gain_block] + [g[half:] for g in proj_got])
    rel = rel.reshape(grid.depth, -1)[:, :gain_len].astype(F32)
    spot = jnp.arange(grid.depth)
    pick = (grid.z + spot[None, :]) % grid.depth == spot[:, None]
    by_shard = jnp.sum(jnp.where(pick[:, :, None], rel[None], 0.0), axis=1)
    wide = by_shard[:, : 4 * rows].reshape(grid.depth, 4, rows)
    wide = wide.transpose(1, 0, 2).reshape(4, width)
    thin = by_shard[:, 4 * rows :].reshape(grid.depth, 2, -1)
    thin = thin.transpose(1, 0, 2).reshape(2, kd)
    gains = jnp.concatenate(
        [wide, jnp.pad(thin, ((0, 2), (0, width - kd)))], axis=0
    )

    device = lax.axis_index(ALL)
    glob_index = device * n + jnp.arange(-2 * n, n, dtype=jnp.int32)
    segment, position = places(glob_index, seq_lengths)
    own_glob = glob_index[2 * n :]
    own_seg = segment[2 * n :]
    cos, sin = turning(position, HEAD_DIM)
    allowed = (
        (segment[None, :] == own_seg[:, None])
        & (glob_index[None, :] <= own_glob[:, None])
        & (own_glob[:, None] - glob_index[None, :] < WINDOW)
        & (glob_index[None, :] >= 0)
    )
    bias = jnp.where(allowed, 0.0, NEGATIVE).astype(F32)

    normed, proj, queries, keys, values, attended, lse, w_full = call(
        attend_kernel,
        [
            ((n, width), LOW, VM),
            ((n, qd + kd), F32, VM),
            ((n, qd), LOW, VM),
            ((3 * n, kd), LOW, VM),
            ((3 * n, kd), LOW, VM),
            ((n, qd), LOW, VM),
            ((HEADS, n, 128), F32, VM),
            ((4 * rows, total_cols), LOW, VM),
        ],
        [SM] + [VM] * 7 + [AN] * 11,
        (
            coords, tokens, near_tok, far_tok, gains, cos, sin, bias,
            w_query, w_key, w_value, *proj_pieces,
        ),
        [dma],
        "attend",
        1_700_000_000,
        9_000_000,
    )

    six = lambda r, c: [
        (((2, 4, r, c) if i == 0 else (4, r, c)), LOW, AN) for i in (0, 1, 2, 0, 1, 2)
    ]
    found = call(
        ffn_kernel,
        [
            ((n, width), LOW, VM),
            ((n, width), F32, VM),
            ((n, qd), LOW, VM),
            ((8, width), F32, VM),
        ]
        + six(half, 2 * fc)
        + six(row_part, width),
        [SM] + [VM] * 4 + [AN] * 20,
        (
            coords, tokens, cotangent, attended, gains,
            w_out, w_down, w_gate, w_up, *row_pieces, *pair_pieces,
        ),
        [
            pltpu.VMEM((4 * out_rows, width), LOW),
            pltpu.VMEM((4 * down_rows, width), LOW),
            pltpu.VMEM((4 * rows, 2 * ff), LOW),
            pltpu.VMEM((4 * out_rows, width), LOW),
            pltpu.VMEM((4 * down_rows, width), LOW),
            pltpu.VMEM((4 * rows, 2 * ff), LOW),
            pltpu.VMEM((n, width), LOW),
            pltpu.VMEM((n, ff), F32),
            pltpu.VMEM((n, ff), F32),
            pltpu.VMEM((n, ff), LOW),
            dma((6,)),
        ],
        "ffn",
        7_000_000_000,
        20_000_000,
    )
    block_out, d_res, d_att, ffn_gains = found[:4]
    pair_sum = gathered_sum(grid, found[4:10])
    row_sum = gathered_sum(grid, found[10:16])

    d_query, near_d, far_d, own_d, q_gain = call(
        attend_back_kernel,
        [
            ((n, qd), LOW, VM),
            ((n, 2 * kd), LOW, VM),
            ((n, 2 * kd), LOW, VM),
            ((n, 2 * kd), F32, VM),
            ((8, kd), F32, VM),
        ],
        [VM] * 10,
        (queries, keys, values, d_att, lse, bias, proj, cos, sin, gains),
        [pltpu.VMEM((3 * n, kd), F32), pltpu.VMEM((3 * n, kd), F32)],
        "attend_back",
        2_000_000_000,
        7_000_000,
    )
    near_back = shifted(near_d, -1)
    far_back = shifted(far_d, -2)
    found = call(
        proj_back_kernel,
        [((n, width), LOW, VM)] + six(half + 16, cols),
        [SM] + [VM] * 14,
        (
            coords, own_d, near_back, far_back, proj, cos, sin, gains,
            d_query, normed, tokens, d_res, w_full, ffn_gains, q_gain,
        ),
        [
            pltpu.VMEM((4 * rows, total_cols), LOW),
            pltpu.VMEM((16, cols), LOW),
            pltpu.VMEM((16, cols), F32),
            dma((2,)),
        ],
        "proj_back",
        1_000_000_000,
        8_000_000,
    )
    tokens_grad = found[0]
    proj_sum = gathered_sum(grid, found[1:7])

    def unpack(kernel, outs, block, scratch, name):
        pieces = spread(grid, block)
        return call(
            kernel, outs, [SM] + [VM] * 8, (coords, *pieces), scratch, name, 0, 4_000_000
        )

    total_gate, total_up = unpack(
        unpack_pair_kernel,
        [((rows, ff), F32, VM), ((rows, ff), F32, VM)],
        pair_sum,
        [],
        "unpack_pair",
    )
    total_out, total_down = unpack(
        unpack_row_kernel,
        [((out_rows, width), F32, VM), ((down_rows, width), F32, VM)],
        row_sum,
        [],
        "unpack_row",
    )
    total_query, total_key, total_value, tail = unpack(
        unpack_proj_kernel,
        [
            ((rows, qd), F32, VM),
            ((rows, kd), F32, VM),
            ((rows, kd), F32, VM),
            ((16, cols), F32, VM),
        ],
        proj_sum,
        [pltpu.VMEM((rows, total_cols), F32)],
        "unpack_proj",
    )
    wide = tail[:8].reshape(4, 2 * cols)[:, :width]
    wide = lax.dynamic_slice_in_dim(wide, grid.z * rows, rows, 1)
    thin = lax.dynamic_slice_in_dim(tail[8:10, :kd], grid.z * (kd // 4), kd // 4, 1)
    return (
        block_out,
        tokens_grad,
        total_query,
        total_key,
        total_value,
        total_out,
        total_gate,
        total_up,
        total_down,
        wide[0],
        thin[0],
        thin[1],
        wide[1],
        wide[2],
        wide[3],
    )


def local(*args):
    w_query, w_out, w_gate, w_down = args[3], args[6], args[7], args[9]
    depth, reps = lax.axis_size("shard"), lax.axis_size("rep")
    aligned = (
        depth == 4
        and reps == 8
        and w_query.shape[0] % 32 == 0
        and w_out.shape[0] % 128 == 0
        and w_down.shape[0] % 128 == 0
        and w_gate.shape[1] % 512 == 0
    )
    return local_fast(*args) if aligned else local_plain(*args)


def solution(mesh):
    rows, cols, vec = P(ALL, None), P("shard", None), P("shard")
    return jax.shard_map(
        local,
        mesh=mesh,
        in_specs=(rows, rows, P()) + (cols,) * 7 + (vec,) * 6,
        out_specs=(rows, rows) + (cols,) * 7 + (vec,) * 6,
        check_vma=False,
    )
```

```python
import functools
import math

import jax
import jax.numpy as jnp
from jax import lax
from jax.experimental import pallas as pl
from jax.experimental.pallas import tpu as pltpu
from jax.sharding import PartitionSpec as P


HEADS = 4
HEAD_DIM = 256
WINDOW = 512
EPS = 1e-06
NEGATIVE = -1e30
ALL = ("rep", "shard")
LOW = jnp.bfloat16
F32 = jnp.float32


class Grid:
    def __init__(self):
        reps = lax.axis_size("rep")
        self.depth = lax.axis_size("shard")
        self.side = math.isqrt(reps // 2)
        assert 2 * self.side * self.side == reps
        rep = lax.axis_index("rep")
        self.z = lax.axis_index("shard")
        if self.side == 2:
            self.core, col, row = rep & 1, (rep >> 1) & 1, rep >> 2
        else:
            self.core = rep % 2
            col = (rep // 2) % self.side
            row = rep // (2 * self.side)
        self.first = jnp.where(self.core == 0, col, row)
        self.second = jnp.where(self.core == 0, row, col)
        self.place = self.second * self.side + self.first

    def pairs(self, move):
        side, depth = self.side, self.depth
        found = []
        for y in range(side):
            for x in range(side):
                for c in range(2):
                    for z in range(depth):
                        ty, tx, tc, tz = move(y, x, c, z)
                        source = ((y * side + x) * 2 + c) * depth + z
                        found.append((source, ((ty * side + tx) * 2 + tc) * depth + tz))
        return found

    def over_first(self, array, by):
        n = self.side
        return lax.ppermute(
            array,
            ALL,
            self.pairs(
                lambda y, x, c, z: (y, (x - by) % n, c, z) if c == 0 else ((y - by) % n, x, c, z)
            ),
        )

    def over_second(self, array, by):
        n = self.side
        return lax.ppermute(
            array,
            ALL,
            self.pairs(
                lambda y, x, c, z: ((y - by) % n, x, c, z) if c == 0 else (y, (x - by) % n, c, z)
            ),
        )

    def over_depth(self, array, by):
        return lax.ppermute(
            array, ALL, self.pairs(lambda y, x, c, z: (y, x, c, (z - by) % self.depth))
        )

    def over_flip(self, array, bits):
        return lax.ppermute(array, ALL, self.pairs(lambda y, x, c, z: (y, x, c, z ^ bits)))

    def over_core(self, array):
        return lax.ppermute(array, ALL, self.pairs(lambda y, x, c, z: (y, x, 1 - c, z)))


def in_order(parts, index):
    n = len(parts)
    if n == 1:
        return list(parts)
    if n == 2:
        own, other = parts
        return [jnp.where(index == 0, own, other), jnp.where(index == 0, other, own)]
    rolled = jnp.roll(jnp.stack(parts), index, axis=0)
    return [rolled[i] for i in range(n)]


def place_shards(parts, z):
    n = len(parts)
    branches = [
        (lambda *a, s=s: jnp.concatenate([a[(m - s) % n] for m in range(n)], axis=0))
        for s in range(n)
    ]
    return lax.switch(z, branches, *parts)


def gather_plane(grid, block):
    n = grid.side
    line = jnp.stack(
        in_order([block] + [grid.over_first(block, k) for k in range(1, n)], grid.first)
    )
    return jnp.stack(
        in_order([line] + [grid.over_second(line, k) for k in range(1, n)], grid.second)
    )


def gather_core(grid, half):
    return in_order([half, grid.over_core(half)], grid.core)


def take(array, index, axis):
    return lax.dynamic_index_in_dim(array, index, axis, keepdims=False)


def add_low(a, *others):
    total = a.astype(F32)
    for b in others:
        total = total + b.astype(F32)
    return total


def reduce_plane(grid, keep, send):
    n = grid.side
    total = add_low(keep, grid.over_core(send)).astype(LOW)
    got = [
        grid.over_first(take(total, (grid.first - k) % n, 2), k) for k in range(1, n)
    ]
    total = add_low(take(total, grid.first, 2), *got).astype(LOW)
    got = [
        grid.over_second(take(total, (grid.second - k) % n, 1), k) for k in range(1, n)
    ]
    return add_low(take(total, grid.second, 1), *got).astype(LOW)


def reduce_depth(grid, total):
    n = grid.depth
    got = [grid.over_depth(take(total, (grid.z - k) % n, 0), k) for k in range(1, n)]
    return add_low(take(total, grid.z, 0), *got)


def shifted(array, by):
    peers = lax.axis_size(ALL)
    pairs = [(i, i + by) for i in range(peers) if 0 <= i + by < peers]
    return lax.ppermute(array, ALL, pairs)


def scaled(vector, scale_gain):
    inv_root = lax.rsqrt(jnp.mean(vector * vector, axis=-1, keepdims=True) + EPS)
    return vector * inv_root * (1.0 + scale_gain)


def places(glob_index, lengths):
    seq_ends = jnp.sum(
        jnp.where(
            jnp.arange(lengths.shape[0])[:, None] >= jnp.arange(lengths.shape[0])[None, :],
            lengths[None, :],
            0,
        ),
        axis=1,
    )
    before = seq_ends[None, :] <= glob_index[:, None]
    segment = jnp.sum(before.astype(jnp.int32), axis=1)
    seq_start = jnp.sum(jnp.where(before, lengths[None, :], 0), axis=1)
    return (segment, glob_index - seq_start)


def turning(position, width):
    half_width = width // 2
    frequency = jnp.exp(
        jnp.arange(half_width, dtype=F32) * (-2.0 * math.log(10000.0) / width)
    )
    angles = position.astype(F32)[:, None] * frequency[None, :]
    return (jnp.cos(angles), jnp.sin(angles))


def rotate(vector, cos_table, sin_table):
    half_width = vector.shape[-1] // 2
    first_half = vector[..., :half_width]
    second_half = vector[..., half_width:]
    return jnp.concatenate(
        [
            first_half * cos_table - second_half * sin_table,
            second_half * cos_table + first_half * sin_table,
        ],
        axis=-1,
    )


def geglu(gate_proj, up_proj):
    return jax.nn.gelu(gate_proj, approximate=True) * up_proj


def matmul(left, right, pattern):
    return jnp.einsum(pattern, left, right, preferred_element_type=F32)


def attend_scores(queries, key_all, allowed):
    scores = matmul(queries, key_all, "qd,kd->qk") * HEAD_DIM ** (-0.5)
    return jnp.where(allowed, scores, NEGATIVE)


def local_plain(
    tokens,
    cotangent,
    seq_lengths,
    w_query,
    w_key,
    w_value,
    w_out,
    w_gate,
    w_up,
    w_down,
    g_in,
    g_query,
    g_key,
    g_post,
    g_pre,
    g_ffn,
):
    grid = Grid()
    depth, side = grid.depth, grid.side
    spots = side * side
    tok_rows, width = tokens.shape
    rows = w_query.shape[0]
    half = rows // 2
    qd, kd = w_query.shape[1], w_key.shape[1]
    out_rows, down_rows, ff = w_out.shape[0], w_down.shape[0], w_gate.shape[1]
    proj_cols = (qd + 2 * kd) // spots
    ff_cols = ff // spots
    out_part, down_part = out_rows // (2 * spots), down_rows // (2 * spots)

    near_tok = shifted(tokens, 1)
    far_tok = shifted(tokens, 2)

    w_proj = jnp.concatenate([w_query, w_key, w_value], axis=1)
    gains_own = jnp.concatenate([g_in, g_post, g_pre, g_ffn, g_query, g_key])
    gain_len = gains_own.shape[0]
    proj_mine = lax.dynamic_slice(
        w_proj, (grid.core * half, grid.place * proj_cols), (half, proj_cols)
    )
    gain_rows = -(-gain_len // (proj_cols * 16)) * 16
    gain_block = jnp.pad(gains_own, (0, gain_rows * proj_cols - gain_len)).reshape(
        gain_rows, proj_cols
    )
    row_mine = jnp.concatenate(
        [
            lax.dynamic_slice_in_dim(
                w_out, (grid.core * spots + grid.place) * out_part, out_part, 0
            ),
            lax.dynamic_slice_in_dim(
                w_down, (grid.core * spots + grid.place) * down_part, down_part, 0
            ),
        ],
        axis=0,
    )
    pair_mine = jnp.concatenate(
        [
            lax.dynamic_slice(w, (grid.core * half, grid.place * ff_cols), (half, ff_cols))
            for w in (w_gate, w_up)
        ],
        axis=1,
    )

    proj_sent = jnp.concatenate([proj_mine, gain_block], axis=0)
    proj_got = [grid.over_depth(proj_sent, k) for k in range(1, depth)]
    row_got = [grid.over_depth(row_mine, k) for k in range(1, depth)]
    pair_got = [grid.over_depth(pair_mine, k) for k in range(1, depth)]

    gains_all = place_shards(
        [gain_block[None]] + [g[None, half:] for g in proj_got], grid.z
    ).reshape(depth, -1)[:, :gain_len].astype(F32)
    gain_sizes = [g.shape[0] for g in (g_in, g_post, g_pre, g_ffn, g_query, g_key)]
    gain_starts = [sum(gain_sizes[:i]) for i in range(len(gain_sizes))]
    gain_in, gain_post, gain_pre, gain_ffn, gain_query, gain_key = [
        gains_all[:, s : s + n].reshape(-1) for s, n in zip(gain_starts, gain_sizes)
    ]

    proj_halves = gather_core(
        grid, gather_plane(grid, jnp.stack([g[:half] for g in proj_got]))
    )
    proj_parts = jnp.stack(proj_halves).transpose(3, 0, 4, 1, 2, 5)
    proj_parts = proj_parts.reshape(depth - 1, rows, qd + 2 * kd)
    proj_full = place_shards(
        [w_proj[None]] + [proj_parts[k : k + 1] for k in range(depth - 1)], grid.z
    ).reshape(depth * rows, qd + 2 * kd)

    row_halves = jnp.stack(gather_core(grid, gather_plane(grid, jnp.stack(row_got))))
    row_halves = row_halves.transpose(3, 0, 1, 2, 4, 5).reshape(
        depth - 1, 2, spots, out_part + down_part, width
    )
    out_parts = row_halves[:, :, :, :out_part].reshape(depth - 1, out_rows, width)
    down_parts = row_halves[:, :, :, out_part:].reshape(depth - 1, down_rows, width)
    out_full = place_shards(
        [w_out[None]] + [out_parts[k : k + 1] for k in range(depth - 1)], grid.z
    ).reshape(depth * out_rows, width)
    down_full = place_shards(
        [w_down[None]] + [down_parts[k : k + 1] for k in range(depth - 1)], grid.z
    ).reshape(depth * down_rows, width)

    pair_own = jnp.stack(
        [w_gate.reshape(rows, spots, ff_cols), w_up.reshape(rows, spots, ff_cols)], axis=2
    ).reshape(rows, 2 * ff)
    pair_parts = jnp.stack(gather_core(grid, gather_plane(grid, jnp.stack(pair_got))))
    pair_parts = pair_parts.transpose(3, 0, 4, 1, 2, 5).reshape(depth - 1, rows, 2 * ff)
    pair_full = place_shards(
        [pair_own[None]] + [pair_parts[k : k + 1] for k in range(depth - 1)], grid.z
    ).reshape(depth * rows, 2 * ff)

    device = lax.axis_index(ALL)
    glob_index = device * tok_rows + jnp.arange(-2 * tok_rows, tok_rows, dtype=jnp.int32)
    segment, position = places(glob_index, seq_lengths)
    own_glob = glob_index[2 * tok_rows :]
    own_seg = segment[2 * tok_rows :]
    cos_all, sin_all = turning(position, HEAD_DIM)
    cos_table, sin_table = cos_all[2 * tok_rows :], sin_all[2 * tok_rows :]
    allowed = (
        (segment[None, :] == own_seg[:, None])
        & (glob_index[None, :] <= own_glob[:, None])
        & (own_glob[:, None] - glob_index[None, :] < WINDOW)
        & (glob_index[None, :] >= 0)
    )
    allowed = jnp.repeat(allowed, HEADS, axis=0)

    def query_side(q_proj, scale_gain):
        return rotate(
            scaled(q_proj.reshape(tok_rows, HEADS, HEAD_DIM), scale_gain),
            cos_table[:, None, :],
            sin_table[:, None, :],
        )

    def key_side(k_proj, scale_gain):
        return rotate(scaled(k_proj, scale_gain), cos_table, sin_table)

    tok_float = tokens.astype(F32)
    normed, in_pull = jax.vjp(scaled, tok_float, gain_in)
    normed_low = normed.astype(LOW)
    halo = jnp.concatenate([far_tok, near_tok], axis=0).astype(F32)
    halo_low = scaled(halo, gain_in).astype(LOW)
    proj_own = matmul(normed_low, proj_full, "tc,cq->tq")
    q_proj = proj_own[:, :qd]
    k_proj = proj_own[:, qd : qd + kd]
    v_proj = proj_own[:, qd + kd :]
    halo_proj = matmul(halo_low, proj_full[:, qd:], "tc,cq->tq")
    halo_keys = rotate(
        scaled(halo_proj[:, :kd], gain_key), cos_all[: 2 * tok_rows], sin_all[: 2 * tok_rows]
    )
    query_val, query_pull = jax.vjp(query_side, q_proj, gain_query)
    queries = query_val.astype(LOW).reshape(tok_rows * HEADS, HEAD_DIM)
    key_val, key_pull = jax.vjp(key_side, k_proj, gain_key)
    key_all = jnp.concatenate([halo_keys, key_val], axis=0).astype(LOW)
    value_all = jnp.concatenate([halo_proj[:, kd:], v_proj], axis=0).astype(LOW)
    scores = attend_scores(queries, key_all, allowed)
    row_max = jnp.max(scores, axis=-1, keepdims=True)
    exponent = jnp.exp(scores - row_max)
    row_total = jnp.sum(exponent, axis=-1, keepdims=True)
    attn_probs = exponent / row_total
    log_total = row_max + jnp.log(row_total)
    attended = matmul(attn_probs.astype(LOW), value_all, "qk,kd->qd")
    attended_low = attended.reshape(tok_rows, HEADS * HEAD_DIM).astype(LOW)
    attn_proj = matmul(attended_low, out_full, "tq,qc->tc")
    post_val, post_pull = jax.vjp(scaled, attn_proj, gain_post)
    residual = tok_float + post_val
    pre_val, pre_pull = jax.vjp(scaled, residual, gain_pre)
    normed_two = pre_val.astype(LOW)
    both = matmul(normed_two, pair_full, "tc,cf->tf").reshape(tok_rows, spots, 2, ff_cols)
    gate_proj, up_proj = both[:, :, 0], both[:, :, 1]
    mixed_val, mixed_pull = jax.vjp(geglu, gate_proj, up_proj)
    mixed_low = mixed_val.astype(LOW).reshape(tok_rows, ff)
    ffn_proj = matmul(mixed_low, down_full, "tf,fc->tc")
    ffn_val, ffn_pull = jax.vjp(scaled, ffn_proj, gain_ffn)
    block_out = (residual + ffn_val).astype(LOW)

    def halves(array, part):
        split = array.reshape(tok_rows, depth, 2, part)
        keep = take(split, grid.core, 2).reshape(tok_rows, depth * part)
        send = take(split, 1 - grid.core, 2).reshape(tok_rows, depth * part)
        return keep, send

    upstream = cotangent.astype(F32)
    d_ffn_proj, d_gain_ffn = ffn_pull(upstream)
    d_ffn_low = d_ffn_proj.astype(LOW)
    mixed_keep, mixed_send = halves(mixed_low, down_part * spots)
    grad_down = [matmul(m, d_ffn_low, "tf,tc->fc").astype(LOW) for m in (mixed_keep, mixed_send)]
    d_mixed = matmul(d_ffn_low, down_full, "tc,fc->tf").reshape(tok_rows, spots, ff_cols)
    d_gate, d_up = mixed_pull(d_mixed)
    d_both = jnp.stack([d_gate.astype(LOW), d_up.astype(LOW)], axis=2).reshape(tok_rows, 2 * ff)
    two_keep, two_send = halves(normed_two, half)
    grad_pair = [matmul(m, d_both, "tc,tf->cf").astype(LOW) for m in (two_keep, two_send)]
    d_normed_two = matmul(d_both, pair_full, "tf,cf->tc")
    d_resid_part, d_gain_pre = pre_pull(d_normed_two)
    d_residual = upstream + d_resid_part
    d_attn_proj, d_gain_post = post_pull(d_residual)
    d_attn_low = d_attn_proj.astype(LOW)
    att_keep, att_send = halves(attended_low, out_part * spots)
    grad_out = [matmul(m, d_attn_low, "tq,tc->qc").astype(LOW) for m in (att_keep, att_send)]

    pair_keep, pair_send = [
        g.reshape(depth, half, side, side, 2 * ff_cols).transpose(0, 2, 3, 1, 4)
        for g in grad_pair
    ]
    pair_sum = reduce_depth(grid, reduce_plane(grid, pair_keep, pair_send))
    row_keep, row_send = [
        jnp.concatenate(
            [
                o.reshape(depth, side, side, out_part, width),
                d.reshape(depth, side, side, down_part, width),
            ],
            axis=3,
        )
        for o, d in zip(grad_out, grad_down)
    ]
    row_sum = reduce_depth(grid, reduce_plane(grid, row_keep, row_send))

    d_attended = (
        matmul(d_attn_low, out_full, "tc,qc->tq")
        .astype(LOW)
        .reshape(tok_rows * HEADS, HEAD_DIM)
    )
    scores_again = attend_scores(queries, key_all, allowed)
    probs_again = jnp.exp(scores_again - log_total)
    d_values_all = matmul(probs_again.astype(LOW), d_attended, "qk,qd->kd")
    d_probs = matmul(d_attended, value_all, "qd,kd->qk")
    d_scores = probs_again * (d_probs - jnp.sum(d_probs * probs_again, axis=-1, keepdims=True))
    d_scores_low = d_scores.astype(LOW)
    d_keys_all = matmul(d_scores_low, queries, "qk,qd->kd") * HEAD_DIM ** (-0.5)
    d_kv_all = jnp.concatenate([d_keys_all, d_values_all], axis=1)
    near_back = shifted(d_kv_all[tok_rows : 2 * tok_rows].astype(LOW), -1)
    far_back = shifted(d_kv_all[:tok_rows].astype(LOW), -2)
    d_queries = matmul(d_scores_low, key_all, "qk,kd->qd") * HEAD_DIM ** (-0.5)
    d_q_proj, d_gain_query = query_pull(d_queries.reshape(tok_rows, HEADS, HEAD_DIM))
    d_kv = add_low(d_kv_all[2 * tok_rows :], near_back, far_back)
    d_k_proj, d_gain_key = key_pull(d_kv[:, :kd])
    d_proj = jnp.concatenate(
        [d_q_proj.astype(LOW), d_k_proj.astype(LOW), d_kv[:, kd:].astype(LOW)], axis=1
    )
    in_keep, in_send = halves(normed_low, half)
    grad_proj = [matmul(m, d_proj, "tc,tq->cq").astype(LOW) for m in (in_keep, in_send)]
    d_normed = matmul(d_proj, proj_full, "tq,cq->tc")
    d_tok_part, d_gain_in = in_pull(d_normed)
    tokens_grad = (d_residual + d_tok_part).astype(LOW)

    proj_keep, proj_send = [
        g.reshape(depth, half, side, side, proj_cols).transpose(0, 2, 3, 1, 4)
        for g in grad_proj
    ]
    proj_sum = reduce_depth(grid, reduce_plane(grid, proj_keep, proj_send))

    d_gains = [d_gain_in, d_gain_post, d_gain_pre, d_gain_ffn, d_gain_query, d_gain_key]
    d_all = jnp.concatenate([g.reshape(depth, -1) for g in d_gains], axis=1)
    lanes = 128
    pad = -(-gain_len // lanes) * lanes - gain_len
    d_all = jnp.pad(d_all, ((0, 0), (0, pad))).reshape(depth, -1, lanes)
    d_all = add_low(d_all, grid.over_core(d_all.astype(LOW)))
    low_all = d_all.astype(LOW)
    d_all = add_low(d_all, *[grid.over_first(low_all, k) for k in range(1, side)])
    low_all = d_all.astype(LOW)
    d_all = add_low(d_all, *[grid.over_second(low_all, k) for k in range(1, side)])
    gain_total = reduce_depth(grid, d_all.astype(LOW)).reshape(-1)
    gain_outs = [gain_total[s : s + n] for s, n in zip(gain_starts, gain_sizes)]

    def whole(block):
        return jnp.stack(gather_core(grid, gather_plane(grid, block.astype(LOW))))

    pair_out = whole(pair_sum).transpose(0, 3, 1, 2, 4).reshape(rows, spots, 2, ff_cols)
    pair_out = pair_out.astype(F32)
    total_gate = pair_out[:, :, 0].reshape(rows, ff)
    total_up = pair_out[:, :, 1].reshape(rows, ff)
    row_out = whole(row_sum).astype(F32)
    total_out = row_out[:, :, :, :out_part].reshape(out_rows, width)
    total_down = row_out[:, :, :, out_part:].reshape(down_rows, width)
    proj_out = whole(proj_sum).transpose(0, 3, 1, 2, 4).reshape(rows, qd + 2 * kd).astype(F32)
    return (
        block_out,
        tokens_grad,
        proj_out[:, :qd],
        proj_out[:, qd : qd + kd],
        proj_out[:, qd + kd :],
        total_out,
        total_gate,
        total_up,
        total_down,
        gain_outs[0],
        gain_outs[4],
        gain_outs[5],
        gain_outs[1],
        gain_outs[2],
        gain_outs[3],
    )


STEPS = ((0, 0), (1, 0), (0, 1), (1, 1))
FLIPS = (0, 2, 1, 3)
NT = (((1,), (1,)), ((), ()))
TN = (((0,), (0,)), ((), ()))
NN = (((1,), (0,)), ((), ()))
GELU_A = math.sqrt(2.0 / math.pi)
GELU_B = 0.044715


def dot(left, right, dims=NN):
    return lax.dot_general(left, right, dims, preferred_element_type=F32)


def spot_of(co, core_side, step):
    core, first, second = co[1], co[2], co[3]
    if core_side == 0:
        half, b1, b2 = core, first, second
    else:
        half, b1, b2 = 1 - core, second, first
    b1 = lax.rem(b1 + step[0], 2)
    b2 = lax.rem(b2 + step[1], 2)
    return half, 2 * b2 + b1


def each_piece(co, refs):
    for side in range(2):
        for i, step in enumerate(STEPS):
            half, place = spot_of(co, side, step)
            yield refs[4 * side + i], half, place


def at_rows(start, size, tile=16):
    return pl.ds(pl.multiple_of(start, tile), size)


def run_all(copies):
    for copy in copies:
        copy.start()


def wait_all(copies):
    for copy in copies:
        copy.wait()


def root_of(v):
    return lax.rsqrt(jnp.mean(v * v, axis=-1, keepdims=True) + EPS)


def norm_back(v, root, gain_one, dy):
    u = dy * gain_one
    dv = root * u - v * (root * root * root) * jnp.mean(u * v, axis=-1, keepdims=True)
    return dv, jnp.sum(dy * v * root, axis=0, keepdims=True)


def turn(v, cos, sin):
    h = v.shape[-1] // 2
    a, b = v[:, :h], v[:, h:]
    return jnp.concatenate([a * cos - b * sin, b * cos + a * sin], axis=-1)


def turn_back(v, cos, sin):
    h = v.shape[-1] // 2
    a, b = v[:, :h], v[:, h:]
    return jnp.concatenate([a * cos + b * sin, b * cos - a * sin], axis=-1)


VM = pl.BlockSpec(memory_space=pltpu.VMEM)
SM = pl.BlockSpec(memory_space=pltpu.SMEM)
AN = pl.BlockSpec(memory_space=pl.ANY)


GRANT = {
    "pk": 60,
    "at": 60,
    "ff": 60,
    "ab": 20,
    "qb": 10,
    "pb": 16,
    "u0": 12,
    "u1": 12,
    "ur": 10,
    "up": 8,
}


def call(kernel, outs, ins, args, scratch, name, flops, moved, aliases=None):
    made = pl.pallas_call(
        kernel,
        out_shape=[jax.ShapeDtypeStruct(s, d) for s, d, _ in outs],
        in_specs=ins,
        out_specs=[m for _, _, m in outs],
        scratch_shapes=scratch,
        input_output_aliases=aliases or {},
        cost_estimate=pl.CostEstimate(flops=flops, bytes_accessed=moved, transcendentals=0),
        compiler_params=pltpu.CompilerParams(vmem_limit_bytes=GRANT[name] * 1024 * 1024),
    )
    return made(*args)


def pack_kernel(
    co, w_query, w_key, w_value, w_out, w_down, w_gate, w_up, proj_o, row_o, pair_o,
    sems, sem,
):
    core, place = co[1], 2 * co[3] + co[2]
    half, cols = w_query.shape[0] // 2, proj_o.shape[1]
    ff_cols = pair_o.shape[1] // 2
    out_part = w_out.shape[0] // 8
    down_part = w_down.shape[0] // 8
    rows = at_rows(core * half, half)
    spot = core * 4 + place
    copies = [
        (w_out.at[at_rows(spot * out_part, out_part)], row_o.at[pl.ds(0, out_part)]),
        (w_down.at[at_rows(spot * down_part, down_part)], row_o.at[pl.ds(out_part, down_part)]),
        (
            w_gate.at[rows, at_rows(place * ff_cols, ff_cols, 128)],
            pair_o.at[:, pl.ds(0, ff_cols)],
        ),
        (
            w_up.at[rows, at_rows(place * ff_cols, ff_cols, 128)],
            pair_o.at[:, pl.ds(ff_cols, ff_cols)],
        ),
    ]
    copies = [pltpu.make_async_copy(s, d, sems.at[i]) for i, (s, d) in enumerate(copies)]
    run_all(copies)
    for p in range(4):

        @pl.when(place == p)
        def _():
            start, found = 0, []
            for w in (w_query, w_key, w_value):
                low = max(p * cols, start)
                high = min((p + 1) * cols, start + w.shape[1])
                if low < high:
                    found.append(
                        pltpu.make_async_copy(
                            w.at[rows, pl.ds(low - start, high - low)],
                            proj_o.at[:, pl.ds(low - p * cols, high - low)],
                            sem,
                        )
                    )
                start += w.shape[1]
            run_all(found)
            wait_all(found)

    wait_all(copies)


def gains_of(co, blocks, rows, thin_rows, width, thin_width):
    lanes = blocks[0].shape[1]
    wide, thin = 0.0, 0.0
    for k, block in enumerate(blocks):
        shard = co[0] ^ k
        values = block[...]
        for n, total in ((rows, width), (thin_rows, thin_width)):
            lane = lax.broadcasted_iota(jnp.int32, (lanes, total), 0)
            spot = lax.broadcasted_iota(jnp.int32, (lanes, total), 1) - shard * n
            pick = jnp.where((lane == spot) & (lane < n), 1.0, 0.0).astype(LOW)
            part = dot(values, pick)
            if total == width:
                wide = wide + part
            else:
                thin = thin + part
    return wide, thin


def attend_kernel(
    co, tok, near, far, own_block, block_1, block_2, block_3, cos, sin, bias,
    w_query, w_key, w_value, *rest,
):
    pieces = rest[:8]
    normed_o, proj_o, key_proj_o, queries_o, keys_o, values_o = rest[8:14]
    attended_o, lse_o, w_o, gains, sem = rest[14:]
    z = co[0]
    n = tok.shape[0]
    rows, qd = w_query.shape
    kd = w_key.shape[1]
    half = rows // 2
    cols = pieces[0].shape[2]
    own = at_rows(z * rows, rows)
    copies = [
        (w_query, w_o.at[own, pl.ds(0, qd)]),
        (w_key, w_o.at[own, pl.ds(qd, kd)]),
        (w_value, w_o.at[own, pl.ds(qd + kd, kd)]),
    ]
    for ref, side, place in each_piece(co, pieces):
        for k in range(3):
            shard = z ^ (k + 1)
            copies.append(
                (
                    ref.at[k],
                    w_o.at[
                        at_rows(shard * rows + side * half, half),
                        at_rows(place * cols, cols, 128),
                    ],
                )
            )
    copies = [pltpu.make_async_copy(s, d, sem) for s, d in copies]
    run_all(copies)
    blocks = (own_block, block_1, block_2, block_3)
    wide, thin = gains_of(co, blocks, rows, kd // 4, tok.shape[1], kd)
    gains[...] = wide
    gains[4:6, :kd] = thin[4:6, :]
    gain_in = 1.0 + gains[0:1, :]
    gain_query = 1.0 + gains[4:5, :HEAD_DIM]
    gain_key = 1.0 + gains[5:6, :HEAD_DIM]

    def normed_of(ref):
        v = ref[...].astype(F32)
        return (v * root_of(v) * gain_in).astype(LOW)

    low = normed_of(tok)
    normed_o[...] = low
    halo = [normed_of(far), normed_of(near)]
    wait_all(copies)
    proj = dot(low, w_o[...])
    proj_o[...] = proj[:, :qd]
    key_proj_o[...] = proj[:, qd : qd + kd]
    for i in range(3):
        kv = proj[:, qd:] if i == 2 else dot(halo[i], w_o[:, qd:])
        at = slice(i * n, (i + 1) * n)
        k = kv[:, :kd]
        k = turn(k * root_of(k) * gain_key, cos[at, :], sin[at, :])
        keys_o[at, :] = k.astype(LOW)
        values_o[at, :] = kv[:, kd:].astype(LOW)
    own_cos, own_sin = cos[2 * n :, :], sin[2 * n :, :]
    for h in range(HEADS):
        at = slice(h * HEAD_DIM, (h + 1) * HEAD_DIM)
        q = proj[:, at]
        q = turn(q * root_of(q) * gain_query, own_cos, own_sin).astype(LOW)
        queries_o[:, at] = q
        scores = dot(q, keys_o[...], NT) * HEAD_DIM ** (-0.5) + bias[...]
        top = jnp.max(scores, axis=-1, keepdims=True)
        e = jnp.exp(scores - top)
        total = jnp.sum(e, axis=-1, keepdims=True)
        p = e / total
        lse_o[h] = jnp.broadcast_to(top + jnp.log(total), lse_o.shape[1:])
        attended_o[:, at] = dot(p.astype(LOW), values_o[...]).astype(LOW)


def out_copies(co, grad, row_of, size, cols_of, refs, sem, dst_rows=None):
    z = co[0]
    found = []
    for side in range(2):
        late, mid, last = refs[3 * side : 3 * side + 3]
        for step in STEPS:
            half, place = spot_of(co, side, step)
            for k, flip in enumerate(FLIPS):
                shard = z ^ flip
                target = late.at[step[1], k] if step[0] else (mid if step[1] else last).at[k]
                if dst_rows is not None:
                    target = target.at[dst_rows]
                source = grad
                if row_of is not None:
                    source = grad.at[at_rows(row_of(shard, half, place), size)]
                    if cols_of is not None:
                        width = cols_of
                        source = grad.at[
                            at_rows(row_of(shard, half, place), size),
                            at_rows(place * width, width, 128),
                        ]
                found.append(pltpu.make_async_copy(source, target, sem))
    return found


def ffn_kernel(co, tok, cot, att, gains, w_out, w_down, w_gate, w_up, *rest):
    row_pieces, pair_pieces = rest[:8], rest[8:16]
    block_o, resid_o, d_att_o, gain_o = rest[16:20]
    pair_refs, row_refs = rest[20:26], rest[26:32]
    (
        out_w,
        down_w,
        pair_w,
        out_g,
        down_g,
        pair_g,
        two_s,
        act_s,
        back_s,
        mixed_s,
        sems,
    ) = rest[32:]
    z = co[0]
    out_rows, down_rows = w_out.shape[0], w_down.shape[0]
    rows, ff = w_gate.shape
    half = rows // 2
    fc = ff // 4
    out_part, down_part = out_rows // 8, down_rows // 8

    def copies_of(pairs, sem):
        return [pltpu.make_async_copy(s, d, sem) for s, d in pairs]

    into_out = [(w_out, out_w.at[at_rows(z * out_rows, out_rows)])]
    into_down = [(w_down, down_w.at[at_rows(z * down_rows, down_rows)])]
    for ref, side, place in each_piece(co, row_pieces):
        for k in range(3):
            shard = z ^ (k + 1)
            spot = side * 4 + place
            into_out.append(
                (
                    ref.at[k, pl.ds(0, out_part)],
                    out_w.at[at_rows(shard * out_rows + spot * out_part, out_part)],
                )
            )
            into_down.append(
                (
                    ref.at[k, pl.ds(out_part, down_part)],
                    down_w.at[at_rows(shard * down_rows + spot * down_part, down_part)],
                )
            )
    into_pair = []
    for q in range(4):
        for i, w in enumerate((w_gate, w_up)):
            into_pair.append(
                (
                    w.at[:, pl.ds(q * fc, fc)],
                    pair_w.at[at_rows(z * rows, rows), pl.ds((2 * q + i) * fc, fc)],
                )
            )
    for ref, side, place in each_piece(co, pair_pieces):
        for k in range(3):
            shard = z ^ (k + 1)
            into_pair.append(
                (
                    ref.at[k],
                    pair_w.at[
                        at_rows(shard * rows + side * half, half),
                        at_rows(place * 2 * fc, 2 * fc, 128),
                    ],
                )
            )
    into_out = copies_of(into_out, sems.at[0])
    into_pair = copies_of(into_pair, sems.at[1])
    into_down = copies_of(into_down, sems.at[2])
    run_all(into_out)
    run_all(into_pair)
    run_all(into_down)

    gain_post = 1.0 + gains[1:2, :]
    gain_pre = 1.0 + gains[2:3, :]
    gain_ffn = 1.0 + gains[3:4, :]
    wait_all(into_out)
    attn = dot(att[...], out_w[...])
    attn_root = root_of(attn)
    residual = tok[...].astype(F32) + attn * attn_root * gain_post
    res_root = root_of(residual)
    two_s[...] = (residual * res_root * gain_pre).astype(LOW)
    wait_all(into_pair)
    wait_all(into_down)
    ffn = None
    for q in range(4):
        both = dot(two_s[...], pair_w[:, 2 * q * fc : 2 * (q + 1) * fc])
        gate, up = both[:, :fc], both[:, fc:]
        t = jnp.tanh(GELU_A * (gate + GELU_B * gate * gate * gate))
        act = 0.5 * gate * (1.0 + t)
        slope = 0.5 * (1.0 + t) + 0.5 * gate * (1.0 - t * t) * (
            GELU_A * (1.0 + 3.0 * GELU_B * gate * gate)
        )
        at = slice(q * fc, (q + 1) * fc)
        act_s[:, at] = act
        back_s[:, at] = up * slope
        mixed = (act * up).astype(LOW)
        mixed_s[:, at] = mixed
        part = dot(mixed, down_w[at, :])
        ffn = part if ffn is None else ffn + part
    ffn_root = root_of(ffn)
    block_o[...] = (residual + ffn * ffn_root * gain_ffn).astype(LOW)

    upstream = cot[...].astype(F32)
    d_ffn, d_gain_ffn = norm_back(ffn, ffn_root, gain_ffn, upstream)
    d_ffn = d_ffn.astype(LOW)
    d_two = None
    for q in range(4):
        at = slice(q * fc, (q + 1) * fc)
        d_mixed = dot(d_ffn, down_w[at, :], NT)
        down_g[at, :] = dot(mixed_s[:, at], d_ffn, TN).astype(LOW)
        d_both = jnp.concatenate(
            [d_mixed * back_s[:, at], d_mixed * act_s[:, at]], axis=1
        ).astype(LOW)
        wide = slice(2 * q * fc, 2 * (q + 1) * fc)
        pair_g[:, wide] = dot(two_s[...], d_both, TN).astype(LOW)
        part = dot(d_both, pair_w[:, wide], NT)
        d_two = part if d_two is None else d_two + part
    pair_copies = out_copies(
        co,
        pair_g,
        lambda shard, side, place: shard * rows + side * half,
        half,
        2 * fc,
        pair_refs,
        sems.at[3],
    )
    down_copies = out_copies(
        co,
        down_g,
        lambda shard, side, place: shard * down_rows + (side * 4 + place) * down_part,
        down_part,
        None,
        row_refs,
        sems.at[4],
        pl.ds(out_part, down_part),
    )
    run_all(pair_copies)
    run_all(down_copies)
    d_res, d_gain_pre = norm_back(residual, res_root, gain_pre, d_two)
    d_res = upstream + d_res
    resid_o[...] = d_res
    d_attn, d_gain_post = norm_back(attn, attn_root, gain_post, d_res)
    d_attn = d_attn.astype(LOW)
    out_g[...] = dot(att[...], d_attn, TN).astype(LOW)
    outer_copies = out_copies(
        co,
        out_g,
        lambda shard, side, place: shard * out_rows + (side * 4 + place) * out_part,
        out_part,
        None,
        row_refs,
        sems.at[5],
        pl.ds(0, out_part),
    )
    run_all(outer_copies)
    d_att_o[...] = dot(d_attn, out_w[...], NT).astype(LOW)
    gain_o[0:1, :] = d_gain_post
    gain_o[1:2, :] = d_gain_pre
    gain_o[2:3, :] = d_gain_ffn
    gain_o[3:, :] = jnp.zeros_like(gain_o[3:, :])
    wait_all(pair_copies)
    wait_all(down_copies)
    wait_all(outer_copies)


def attend_back_kernel(
    queries, keys, values, d_att, lse, bias, proj, cos, sin, gains,
    d_query_o, near_o, far_o, own_o, gain_o, d_keys, d_values,
):
    n = queries.shape[0]
    kd = keys.shape[1]
    unit = HEAD_DIM ** (-0.5)
    gain_query = 1.0 + gains[4:5, :HEAD_DIM]
    own_cos, own_sin = cos[2 * n :, :], sin[2 * n :, :]
    gain_sum = None
    for h in range(HEADS):
        at = slice(h * HEAD_DIM, (h + 1) * HEAD_DIM)
        q, da = queries[:, at], d_att[:, at]
        scores = dot(q, keys[...], NT) * unit + bias[...]
        p = jnp.exp(scores - lse[h][:, :1])
        d_p = dot(da, values[...], NT)
        d_s = (p * (d_p - jnp.sum(d_p * p, axis=-1, keepdims=True))).astype(LOW)
        d_v = dot(p.astype(LOW), da, TN)
        d_k = dot(d_s, q, TN)
        if h == 0:
            d_values[...] = d_v
            d_keys[...] = d_k
        else:
            d_values[...] += d_v
            d_keys[...] += d_k
        d_q = turn_back(dot(d_s, keys[...]) * unit, own_cos, own_sin)
        v = proj[:, at]
        d_v_q, d_gain = norm_back(v, root_of(v), gain_query, d_q)
        d_query_o[:, at] = d_v_q.astype(LOW)
        gain_sum = d_gain if gain_sum is None else gain_sum + d_gain
    gain_o[...] = jnp.broadcast_to(gain_sum, gain_o.shape)
    for ref, start in ((far_o, 0), (near_o, n), (own_o, 2 * n)):
        ref[:, :kd] = (d_keys[start : start + n, :] * unit).astype(ref.dtype)
        ref[:, kd:] = d_values[start : start + n, :].astype(ref.dtype)


def query_back_kernel(d_query, normed, w, grad_o, part_o):
    grad_o[...] = dot(normed[...], d_query[...], TN).astype(LOW)
    part_o[...] = dot(d_query[...], w[:, : d_query.shape[1]], NT)


def proj_back_kernel(
    co, own, near, far, key_proj, cos, sin, gains, query_part, normed, tok, d_res, ffn_gains,
    q_gain, w, query_grad, tokens_o, *rest,
):
    refs, (grad, low_tail, tail, w_kv, sems) = rest[:6], rest[6:]
    n, width = tok.shape
    kd = key_proj.shape[1]
    qd = query_grad.shape[1]
    rows = w.shape[0] // 4
    half = rows // 2
    cols = w.shape[1] // 4
    loads = [
        pltpu.make_async_copy(w.at[:, pl.ds(qd, 2 * kd)], w_kv, sems.at[2]),
        pltpu.make_async_copy(query_grad, grad.at[:, pl.ds(0, qd)], sems.at[3]),
    ]
    run_all(loads)
    d_kv = own[...] + near[...].astype(F32) + far[...].astype(F32)
    gain_key = 1.0 + gains[5:6, :kd]
    gain_in = 1.0 + gains[0:1, :]
    v = key_proj[...]
    d_k = turn_back(d_kv[:, :kd], cos[2 * n :, :], sin[2 * n :, :])
    d_k, d_gain_key = norm_back(v, root_of(v), gain_key, d_k)
    d_proj = jnp.concatenate([d_k.astype(LOW), d_kv[:, kd:].astype(LOW)], axis=1)
    grad[:, qd:] = dot(normed[...], d_proj, TN).astype(LOW)
    wait_all(loads)
    copies = out_copies(
        co,
        grad,
        lambda shard, side, place: shard * rows + side * half,
        half,
        cols,
        refs,
        sems.at[0],
        pl.ds(0, half),
    )
    run_all(copies)
    d_normed = query_part[...] + dot(d_proj, w_kv[...], NT)
    x = tok[...].astype(F32)
    d_x, d_gain_in = norm_back(x, root_of(x), gain_in, d_normed)
    tokens_o[...] = (d_res[...] + d_x).astype(LOW)
    tail[...] = jnp.zeros_like(tail)
    parts = [d_gain_in, ffn_gains[0:1, :], ffn_gains[1:2, :], ffn_gains[2:3, :]]
    for i, part in enumerate(parts):
        tail[2 * i : 2 * i + 1, :] = part[:, :cols]
        tail[2 * i + 1 : 2 * i + 2, : width - cols] = part[:, cols:]
    tail[8:9, :kd] = q_gain[0:1, :]
    tail[9:10, :kd] = d_gain_key
    low_tail[...] = tail[...].astype(LOW)
    tail_rows = low_tail.shape[0]
    more = out_copies(
        co, low_tail, None, None, None, refs, sems.at[1], pl.ds(half, tail_rows)
    )
    run_all(more)
    wait_all(copies)
    wait_all(more)


def unpack_pair_kernel(core_side, co, *rest):
    pieces = rest[:4]
    gate_o, up_o, wide, sem = rest[-4:]
    half = gate_o.shape[0] // 2
    fc = gate_o.shape[1] // 4
    copies = []
    for i, step in enumerate(STEPS):
        side, place = spot_of(co, core_side, step)
        wide[i] = pieces[i][...].astype(F32)
        at = (at_rows(side * half, half), at_rows(place * fc, fc, 128))
        found = [
            pltpu.make_async_copy(wide.at[i, :, pl.ds(0, fc)], gate_o.at[at], sem),
            pltpu.make_async_copy(wide.at[i, :, pl.ds(fc, fc)], up_o.at[at], sem),
        ]
        run_all(found)
        copies += found
    wait_all(copies)


def unpack_row_kernel(co, *rest):
    pieces, (out_o, down_o) = rest[:8], rest[8:]
    out_part, down_part = out_o.shape[0] // 8, down_o.shape[0] // 8
    for ref, side, place in each_piece(co, pieces):
        spot = side * 4 + place
        out_o[at_rows(spot * out_part, out_part), :] = ref[:out_part, :].astype(F32)
        down_o[at_rows(spot * down_part, down_part), :] = ref[out_part:, :].astype(F32)


def unpack_proj_kernel(co, *rest):
    pieces, (query_o, key_o, value_o, tail_o, full) = rest[:8], rest[8:]
    half = query_o.shape[0] // 2
    cols = full.shape[1] // 4
    qd, kd = query_o.shape[1], key_o.shape[1]
    for ref, side, place in each_piece(co, pieces):
        full[at_rows(side * half, half), at_rows(place * cols, cols, 128)] = ref[
            :half, :
        ].astype(F32)
    query_o[...] = full[:, :qd]
    key_o[...] = full[:, qd : qd + kd]
    value_o[...] = full[:, qd + kd :]
    tail_o[...] = pieces[0][half:, :].astype(F32)


def spread(grid, block):
    own = [block]
    own.append(grid.over_first(block, 1))
    own.append(grid.over_second(block, 1))
    own.append(grid.over_second(own[1], 1))
    return own + [grid.over_core(b) for b in own]


def along_depth(grid, block):
    two = grid.over_flip(block, 2)
    one = grid.over_flip(block, 1)
    return [one, two, grid.over_flip(two, 1)]


def after(value, *others):
    return lax.optimization_barrier((value, *others))[0]


def first_sum(grid, arrays, wait=()):
    keep_late, keep_mid, keep_last, send_late, send_mid, send_last = arrays
    late_got = grid.over_core(send_late)
    mid_got = grid.over_core(send_mid)
    last_got = grid.over_core(send_last)
    if wait:
        keep_late = after(keep_late, *wait)
    late = add_low(keep_late, late_got).astype(LOW)
    first_got = grid.over_first(late, 1)
    return (keep_last, last_got, first_got[0]), (keep_mid, mid_got, first_got[1])


def second_sum(begun, wait=()):
    parts, (keep_mid, mid_got, first_got) = begun
    if wait:
        keep_mid = after(keep_mid, *wait)
    return parts, add_low(keep_mid, mid_got, first_got).astype(LOW)


def plane_sums(grid, begun, wait=()):
    parts, mid = begun
    parts = (*parts, grid.over_second(mid, 1))
    if wait:
        parts = (after(parts[0], *wait), *parts[1:])
    return parts, add_low(*[p[2:] for p in parts]).astype(LOW)


def depth_sum(grid, sums):
    parts, away = sums
    got = grid.over_flip(away, 1)
    far = add_low(*[p[1] for p in parts], got[1]).astype(LOW)
    far_got = grid.over_flip(far, 2)
    return add_low(*[p[0] for p in parts], got[0], far_got).astype(LOW)


def local_fast(
    tokens,
    cotangent,
    seq_lengths,
    w_query,
    w_key,
    w_value,
    w_out,
    w_gate,
    w_up,
    w_down,
    g_in,
    g_query,
    g_key,
    g_post,
    g_pre,
    g_ffn,
):
    grid = Grid()
    n, width = tokens.shape
    rows, qd = w_query.shape
    kd = w_key.shape[1]
    half = rows // 2
    out_rows, down_rows, ff = w_out.shape[0], w_down.shape[0], w_gate.shape[1]
    total_cols = qd + 2 * kd
    cols, fc = total_cols // 4, ff // 4
    out_part, down_part = out_rows // 8, down_rows // 8
    row_part = out_part + down_part
    coords = jnp.stack([grid.z, grid.core, grid.first, grid.second]).astype(jnp.int32)
    dma = pltpu.SemaphoreType.DMA

    proj_mine, row_mine, pair_mine = call(
        pack_kernel,
        [
            ((half, cols), LOW, VM),
            ((row_part, width), LOW, VM),
            ((half, 2 * fc), LOW, VM),
        ],
        [SM] + [AN] * 7,
        (coords, w_query, w_key, w_value, w_out, w_down, w_gate, w_up),
        [dma((4,)), dma],
        "pk",
        0,
        2_000_000,
    )
    device = lax.axis_index(ALL)
    seq_lengths = after(seq_lengths, proj_mine)
    glob_index = device * n + jnp.arange(-2 * n, n, dtype=jnp.int32)
    segment, position = places(glob_index, seq_lengths)
    own_glob = glob_index[2 * n :]
    own_seg = segment[2 * n :]
    cos, sin = turning(position, HEAD_DIM)
    allowed = (
        (segment[None, :] == own_seg[:, None])
        & (glob_index[None, :] <= own_glob[:, None])
        & (own_glob[:, None] - glob_index[None, :] < WINDOW)
        & (glob_index[None, :] >= 0)
    )
    bias = jnp.where(allowed, 0.0, NEGATIVE).astype(F32)

    gains_late = after((g_in, g_post, g_pre, g_ffn, g_query, g_key), proj_mine)
    gain_block = jnp.zeros((16, cols), LOW)
    for i, g in enumerate(gains_late):
        gain_block += jnp.pad(g[None], ((i, 15 - i), (0, cols - g.shape[0])))
    gain_got = [grid.over_flip(gain_block, k) for k in range(1, grid.depth)]
    tokens_late = lax.optimization_barrier((tokens, proj_mine))[0]
    proj_got = along_depth(grid, proj_mine)
    row_got = along_depth(grid, row_mine)
    pair_got = along_depth(grid, pair_mine)
    near_tok = shifted(tokens_late, 1)
    far_tok = shifted(near_tok, 1)
    proj_pieces = spread(grid, jnp.stack(proj_got))
    row_pieces = spread(grid, jnp.stack(row_got))
    pair_pieces = spread(grid, jnp.stack(pair_got))

    normed, proj, key_proj, queries, keys, values, attended, lse, w_full, gains = call(
        attend_kernel,
        [
            ((n, width), LOW, VM),
            ((n, qd), F32, VM),
            ((n, kd), F32, VM),
            ((n, qd), LOW, VM),
            ((3 * n, kd), LOW, VM),
            ((3 * n, kd), LOW, VM),
            ((n, qd), LOW, VM),
            ((HEADS, n, 128), F32, VM),
            ((4 * rows, total_cols), LOW, VM),
            ((16, width), F32, VM),
        ],
        [SM] + [VM] * 10 + [AN] * 11,
        (
            coords, tokens, near_tok, far_tok, gain_block, *gain_got, cos, sin, bias,
            w_query, w_key, w_value, *proj_pieces,
        ),
        [dma],
        "at",
        1_700_000_000,
        9_000_000,
    )

    six = lambda r, c: [
        (((2, 4, r, c) if i == 0 else (4, r, c)), LOW, AN) for i in (0, 1, 2, 0, 1, 2)
    ]
    found = call(
        ffn_kernel,
        [
            ((n, width), LOW, VM),
            ((n, width), F32, VM),
            ((n, qd), LOW, VM),
            ((8, width), F32, VM),
        ]
        + six(half, 2 * fc)
        + six(row_part, width),
        [SM] + [VM] * 4 + [AN] * 20,
        (
            coords, tokens, cotangent, attended, gains,
            w_out, w_down, w_gate, w_up, *row_pieces, *pair_pieces,
        ),
        [
            pltpu.VMEM((4 * out_rows, width), LOW),
            pltpu.VMEM((4 * down_rows, width), LOW),
            pltpu.VMEM((4 * rows, 2 * ff), LOW),
            pltpu.VMEM((4 * out_rows, width), LOW),
            pltpu.VMEM((4 * down_rows, width), LOW),
            pltpu.VMEM((4 * rows, 2 * ff), LOW),
            pltpu.VMEM((n, width), LOW),
            pltpu.VMEM((n, ff), F32),
            pltpu.VMEM((n, ff), F32),
            pltpu.VMEM((n, ff), LOW),
            dma((6,)),
        ],
        "ff",
        7_000_000_000,
        20_000_000,
    )
    block_out, d_res, d_att, ffn_gains = found[:4]
    pair_late = first_sum(grid, found[4:10])
    row_late = first_sum(grid, found[10:16])
    d_query, near_d, far_d, own_d, q_gain = call(
        attend_back_kernel,
        [
            ((n, qd), LOW, VM),
            ((n, 2 * kd), LOW, VM),
            ((n, 2 * kd), LOW, VM),
            ((n, 2 * kd), F32, VM),
            ((8, kd), F32, VM),
        ],
        [VM] * 10,
        (queries, keys, values, d_att, lse, bias, proj, cos, sin, gains),
        [pltpu.VMEM((3 * n, kd), F32), pltpu.VMEM((3 * n, kd), F32)],
        "ab",
        2_000_000_000,
        7_000_000,
    )
    near_back = shifted(near_d, -1)
    far_back = shifted(far_d, -2)
    query_grad, query_part = call(
        query_back_kernel,
        [((4 * rows, qd), LOW, VM), ((n, width), F32, VM)],
        [VM] * 3,
        (d_query, normed, w_full),
        [],
        "qb",
        700_000_000,
        5_000_000,
    )
    pair_begun = second_sum(pair_late)
    row_begun = second_sum(row_late, (query_part,))
    pair_sums = plane_sums(grid, pair_begun, row_begun[1:])
    row_sums = plane_sums(grid, row_begun)
    pair_sum = depth_sum(grid, pair_sums)
    row_sum = depth_sum(grid, row_sums)
    found = call(
        proj_back_kernel,
        [((n, width), LOW, VM)] + six(half + 16, cols),
        [SM] + [VM] * 13 + [AN] * 2,
        (
            coords, own_d, near_back, far_back, key_proj, cos, sin, gains,
            query_part, normed, tokens, d_res, ffn_gains, q_gain, w_full, query_grad,
        ),
        [
            pltpu.VMEM((4 * rows, total_cols), LOW),
            pltpu.VMEM((16, cols), LOW),
            pltpu.VMEM((16, cols), F32),
            pltpu.VMEM((4 * rows, 2 * kd), LOW),
            dma((4,)),
        ],
        "pb",
        400_000_000,
        6_000_000,
    )
    tokens_grad = found[0]
    proj_begun = second_sum(first_sum(grid, found[1:7]))
    proj_sum = depth_sum(grid, plane_sums(grid, proj_begun))

    pieces = spread(grid, pair_sum)
    made = ()
    for core_side in range(2):
        made = call(
            functools.partial(unpack_pair_kernel, core_side),
            [((rows, ff), F32, AN)] * 2,
            [SM] + [VM] * 4 + [AN] * len(made),
            (coords, *pieces[4 * core_side : 4 * core_side + 4], *made),
            [pltpu.VMEM((4, half, 2 * fc), F32), dma],
            "u" + str(core_side),
            0,
            4_000_000,
            {5 + i: i for i in range(len(made))},
        )
    total_gate, total_up = made
    total_out, total_down = call(
        unpack_row_kernel,
        [((out_rows, width), F32, VM), ((down_rows, width), F32, VM)],
        [SM] + [VM] * 8,
        (coords, *spread(grid, row_sum)),
        [],
        "ur",
        0,
        3_000_000,
    )
    total_query, total_key, total_value, tail = call(
        unpack_proj_kernel,
        [
            ((rows, qd), F32, VM),
            ((rows, kd), F32, VM),
            ((rows, kd), F32, VM),
            ((16, cols), F32, VM),
        ],
        [SM] + [VM] * 8,
        (coords, *spread(grid, proj_sum)),
        [pltpu.VMEM((rows, total_cols), F32)],
        "up",
        0,
        2_000_000,
    )
    wide = tail[:8].reshape(4, 2 * cols)[:, :width]
    wide = lax.dynamic_slice_in_dim(wide, grid.z * rows, rows, 1)
    thin = lax.dynamic_slice_in_dim(tail[8:10, :kd], grid.z * (kd // 4), kd // 4, 1)
    return (
        block_out,
        tokens_grad,
        total_query,
        total_key,
        total_value,
        total_out,
        total_gate,
        total_up,
        total_down,
        wide[0],
        thin[0],
        thin[1],
        wide[1],
        wide[2],
        wide[3],
    )


def local(*args):
    w_query, w_out, w_gate, w_down = args[3], args[6], args[7], args[9]
    depth, reps = lax.axis_size("shard"), lax.axis_size("rep")
    aligned = (
        depth == 4
        and reps == 8
        and w_query.shape[0] % 32 == 0
        and w_out.shape[0] % 128 == 0
        and w_down.shape[0] % 128 == 0
        and w_gate.shape[1] % 512 == 0
    )
    if not aligned:
        return local_plain(*args)
    return local_fast(*args)


def solution(mesh):
    rows, cols, vec = P(ALL, None), P("shard", None), P("shard")
    return jax.shard_map(
        local,
        mesh=mesh,
        in_specs=(rows, rows, P()) + (cols,) * 7 + (vec,) * 6,
        out_specs=(rows, rows) + (cols,) * 7 + (vec,) * 6,
        check_vma=False,
    )
```

```python
import functools
import math

import jax
import jax.numpy as jnp
from jax import lax
from jax.experimental import pallas as pl
from jax.experimental.pallas import tpu as pltpu
from jax.sharding import PartitionSpec as P


HEADS = 4
HEAD_DIM = 256
WINDOW = 512
EPS = 1e-06
NEGATIVE = -1e30
ALL = ("rep", "shard")
LOW = jnp.bfloat16
F32 = jnp.float32


class Grid:
    def __init__(self):
        reps = lax.axis_size("rep")
        self.depth = lax.axis_size("shard")
        self.side = math.isqrt(reps // 2)
        assert 2 * self.side * self.side == reps
        rep = lax.axis_index("rep")
        self.z = lax.axis_index("shard")
        if self.side == 2:
            self.core, col, row = rep & 1, (rep >> 1) & 1, rep >> 2
        else:
            self.core = rep % 2
            col = (rep // 2) % self.side
            row = rep // (2 * self.side)
        self.first = jnp.where(self.core == 0, col, row)
        self.second = jnp.where(self.core == 0, row, col)
        self.place = self.second * self.side + self.first

    def pairs(self, move):
        side, depth = self.side, self.depth
        found = []
        for y in range(side):
            for x in range(side):
                for c in range(2):
                    for z in range(depth):
                        ty, tx, tc, tz = move(y, x, c, z)
                        source = ((y * side + x) * 2 + c) * depth + z
                        found.append((source, ((ty * side + tx) * 2 + tc) * depth + tz))
        return found

    def over_first(self, array, by):
        n = self.side
        return lax.ppermute(
            array,
            ALL,
            self.pairs(
                lambda y, x, c, z: (y, (x - by) % n, c, z) if c == 0 else ((y - by) % n, x, c, z)
            ),
        )

    def over_second(self, array, by):
        n = self.side
        return lax.ppermute(
            array,
            ALL,
            self.pairs(
                lambda y, x, c, z: ((y - by) % n, x, c, z) if c == 0 else (y, (x - by) % n, c, z)
            ),
        )

    def over_depth(self, array, by):
        return lax.ppermute(
            array, ALL, self.pairs(lambda y, x, c, z: (y, x, c, (z - by) % self.depth))
        )

    def over_flip(self, array, bits):
        return lax.ppermute(array, ALL, self.pairs(lambda y, x, c, z: (y, x, c, z ^ bits)))

    def over_core(self, array):
        return lax.ppermute(array, ALL, self.pairs(lambda y, x, c, z: (y, x, 1 - c, z)))


def in_order(parts, index):
    n = len(parts)
    if n == 1:
        return list(parts)
    if n == 2:
        own, other = parts
        return [jnp.where(index == 0, own, other), jnp.where(index == 0, other, own)]
    rolled = jnp.roll(jnp.stack(parts), index, axis=0)
    return [rolled[i] for i in range(n)]


def place_shards(parts, z):
    n = len(parts)
    branches = [
        (lambda *a, s=s: jnp.concatenate([a[(m - s) % n] for m in range(n)], axis=0))
        for s in range(n)
    ]
    return lax.switch(z, branches, *parts)


def gather_plane(grid, block):
    n = grid.side
    line = jnp.stack(
        in_order([block] + [grid.over_first(block, k) for k in range(1, n)], grid.first)
    )
    return jnp.stack(
        in_order([line] + [grid.over_second(line, k) for k in range(1, n)], grid.second)
    )


def gather_core(grid, half):
    return in_order([half, grid.over_core(half)], grid.core)


def take(array, index, axis):
    return lax.dynamic_index_in_dim(array, index, axis, keepdims=False)


def add_low(a, *others):
    total = a.astype(F32)
    for b in others:
        total = total + b.astype(F32)
    return total


def reduce_plane(grid, keep, send):
    n = grid.side
    total = add_low(keep, grid.over_core(send)).astype(LOW)
    got = [
        grid.over_first(take(total, (grid.first - k) % n, 2), k) for k in range(1, n)
    ]
    total = add_low(take(total, grid.first, 2), *got).astype(LOW)
    got = [
        grid.over_second(take(total, (grid.second - k) % n, 1), k) for k in range(1, n)
    ]
    return add_low(take(total, grid.second, 1), *got).astype(LOW)


def reduce_depth(grid, total):
    n = grid.depth
    got = [grid.over_depth(take(total, (grid.z - k) % n, 0), k) for k in range(1, n)]
    return add_low(take(total, grid.z, 0), *got)


def shifted(array, by):
    peers = lax.axis_size(ALL)
    pairs = [(i, i + by) for i in range(peers) if 0 <= i + by < peers]
    return lax.ppermute(array, ALL, pairs)


def scaled(vector, scale_gain):
    inv_root = lax.rsqrt(jnp.mean(vector * vector, axis=-1, keepdims=True) + EPS)
    return vector * inv_root * (1.0 + scale_gain)


def places(glob_index, lengths):
    seq_ends = jnp.sum(
        jnp.where(
            jnp.arange(lengths.shape[0])[:, None] >= jnp.arange(lengths.shape[0])[None, :],
            lengths[None, :],
            0,
        ),
        axis=1,
    )
    before = seq_ends[None, :] <= glob_index[:, None]
    segment = jnp.sum(before.astype(jnp.int32), axis=1)
    seq_start = jnp.sum(jnp.where(before, lengths[None, :], 0), axis=1)
    return (segment, glob_index - seq_start)


def turning(position, width):
    half_width = width // 2
    frequency = jnp.exp(
        jnp.arange(half_width, dtype=F32) * (-2.0 * math.log(10000.0) / width)
    )
    angles = position.astype(F32)[:, None] * frequency[None, :]
    return (jnp.cos(angles), jnp.sin(angles))


def rotate(vector, cos_table, sin_table):
    half_width = vector.shape[-1] // 2
    first_half = vector[..., :half_width]
    second_half = vector[..., half_width:]
    return jnp.concatenate(
        [
            first_half * cos_table - second_half * sin_table,
            second_half * cos_table + first_half * sin_table,
        ],
        axis=-1,
    )


def geglu(gate_proj, up_proj):
    return jax.nn.gelu(gate_proj, approximate=True) * up_proj


def matmul(left, right, pattern):
    return jnp.einsum(pattern, left, right, preferred_element_type=F32)


def attend_scores(queries, key_all, allowed):
    scores = matmul(queries, key_all, "qd,kd->qk") * HEAD_DIM ** (-0.5)
    return jnp.where(allowed, scores, NEGATIVE)


def local_plain(
    tokens,
    cotangent,
    seq_lengths,
    w_query,
    w_key,
    w_value,
    w_out,
    w_gate,
    w_up,
    w_down,
    g_in,
    g_query,
    g_key,
    g_post,
    g_pre,
    g_ffn,
):
    grid = Grid()
    depth, side = grid.depth, grid.side
    spots = side * side
    tok_rows, width = tokens.shape
    rows = w_query.shape[0]
    half = rows // 2
    qd, kd = w_query.shape[1], w_key.shape[1]
    out_rows, down_rows, ff = w_out.shape[0], w_down.shape[0], w_gate.shape[1]
    proj_cols = (qd + 2 * kd) // spots
    ff_cols = ff // spots
    out_part, down_part = out_rows // (2 * spots), down_rows // (2 * spots)

    near_tok = shifted(tokens, 1)
    far_tok = shifted(tokens, 2)

    w_proj = jnp.concatenate([w_query, w_key, w_value], axis=1)
    gains_own = jnp.concatenate([g_in, g_post, g_pre, g_ffn, g_query, g_key])
    gain_len = gains_own.shape[0]
    proj_mine = lax.dynamic_slice(
        w_proj, (grid.core * half, grid.place * proj_cols), (half, proj_cols)
    )
    gain_rows = -(-gain_len // (proj_cols * 16)) * 16
    gain_block = jnp.pad(gains_own, (0, gain_rows * proj_cols - gain_len)).reshape(
        gain_rows, proj_cols
    )
    row_mine = jnp.concatenate(
        [
            lax.dynamic_slice_in_dim(
                w_out, (grid.core * spots + grid.place) * out_part, out_part, 0
            ),
            lax.dynamic_slice_in_dim(
                w_down, (grid.core * spots + grid.place) * down_part, down_part, 0
            ),
        ],
        axis=0,
    )
    pair_mine = jnp.concatenate(
        [
            lax.dynamic_slice(w, (grid.core * half, grid.place * ff_cols), (half, ff_cols))
            for w in (w_gate, w_up)
        ],
        axis=1,
    )

    proj_sent = jnp.concatenate([proj_mine, gain_block], axis=0)
    proj_got = [grid.over_depth(proj_sent, k) for k in range(1, depth)]
    row_got = [grid.over_depth(row_mine, k) for k in range(1, depth)]
    pair_got = [grid.over_depth(pair_mine, k) for k in range(1, depth)]

    gains_all = place_shards(
        [gain_block[None]] + [g[None, half:] for g in proj_got], grid.z
    ).reshape(depth, -1)[:, :gain_len].astype(F32)
    gain_sizes = [g.shape[0] for g in (g_in, g_post, g_pre, g_ffn, g_query, g_key)]
    gain_starts = [sum(gain_sizes[:i]) for i in range(len(gain_sizes))]
    gain_in, gain_post, gain_pre, gain_ffn, gain_query, gain_key = [
        gains_all[:, s : s + n].reshape(-1) for s, n in zip(gain_starts, gain_sizes)
    ]

    proj_halves = gather_core(
        grid, gather_plane(grid, jnp.stack([g[:half] for g in proj_got]))
    )
    proj_parts = jnp.stack(proj_halves).transpose(3, 0, 4, 1, 2, 5)
    proj_parts = proj_parts.reshape(depth - 1, rows, qd + 2 * kd)
    proj_full = place_shards(
        [w_proj[None]] + [proj_parts[k : k + 1] for k in range(depth - 1)], grid.z
    ).reshape(depth * rows, qd + 2 * kd)

    row_halves = jnp.stack(gather_core(grid, gather_plane(grid, jnp.stack(row_got))))
    row_halves = row_halves.transpose(3, 0, 1, 2, 4, 5).reshape(
        depth - 1, 2, spots, out_part + down_part, width
    )
    out_parts = row_halves[:, :, :, :out_part].reshape(depth - 1, out_rows, width)
    down_parts = row_halves[:, :, :, out_part:].reshape(depth - 1, down_rows, width)
    out_full = place_shards(
        [w_out[None]] + [out_parts[k : k + 1] for k in range(depth - 1)], grid.z
    ).reshape(depth * out_rows, width)
    down_full = place_shards(
        [w_down[None]] + [down_parts[k : k + 1] for k in range(depth - 1)], grid.z
    ).reshape(depth * down_rows, width)

    pair_own = jnp.stack(
        [w_gate.reshape(rows, spots, ff_cols), w_up.reshape(rows, spots, ff_cols)], axis=2
    ).reshape(rows, 2 * ff)
    pair_parts = jnp.stack(gather_core(grid, gather_plane(grid, jnp.stack(pair_got))))
    pair_parts = pair_parts.transpose(3, 0, 4, 1, 2, 5).reshape(depth - 1, rows, 2 * ff)
    pair_full = place_shards(
        [pair_own[None]] + [pair_parts[k : k + 1] for k in range(depth - 1)], grid.z
    ).reshape(depth * rows, 2 * ff)

    device = lax.axis_index(ALL)
    glob_index = device * tok_rows + jnp.arange(-2 * tok_rows, tok_rows, dtype=jnp.int32)
    segment, position = places(glob_index, seq_lengths)
    own_glob = glob_index[2 * tok_rows :]
    own_seg = segment[2 * tok_rows :]
    cos_all, sin_all = turning(position, HEAD_DIM)
    cos_table, sin_table = cos_all[2 * tok_rows :], sin_all[2 * tok_rows :]
    allowed = (
        (segment[None, :] == own_seg[:, None])
        & (glob_index[None, :] <= own_glob[:, None])
        & (own_glob[:, None] - glob_index[None, :] < WINDOW)
        & (glob_index[None, :] >= 0)
    )
    allowed = jnp.repeat(allowed, HEADS, axis=0)

    def query_side(q_proj, scale_gain):
        return rotate(
            scaled(q_proj.reshape(tok_rows, HEADS, HEAD_DIM), scale_gain),
            cos_table[:, None, :],
            sin_table[:, None, :],
        )

    def key_side(k_proj, scale_gain):
        return rotate(scaled(k_proj, scale_gain), cos_table, sin_table)

    tok_float = tokens.astype(F32)
    normed, in_pull = jax.vjp(scaled, tok_float, gain_in)
    normed_low = normed.astype(LOW)
    halo = jnp.concatenate([far_tok, near_tok], axis=0).astype(F32)
    halo_low = scaled(halo, gain_in).astype(LOW)
    proj_own = matmul(normed_low, proj_full, "tc,cq->tq")
    q_proj = proj_own[:, :qd]
    k_proj = proj_own[:, qd : qd + kd]
    v_proj = proj_own[:, qd + kd :]
    halo_proj = matmul(halo_low, proj_full[:, qd:], "tc,cq->tq")
    halo_keys = rotate(
        scaled(halo_proj[:, :kd], gain_key), cos_all[: 2 * tok_rows], sin_all[: 2 * tok_rows]
    )
    query_val, query_pull = jax.vjp(query_side, q_proj, gain_query)
    queries = query_val.astype(LOW).reshape(tok_rows * HEADS, HEAD_DIM)
    key_val, key_pull = jax.vjp(key_side, k_proj, gain_key)
    key_all = jnp.concatenate([halo_keys, key_val], axis=0).astype(LOW)
    value_all = jnp.concatenate([halo_proj[:, kd:], v_proj], axis=0).astype(LOW)
    scores = attend_scores(queries, key_all, allowed)
    row_max = jnp.max(scores, axis=-1, keepdims=True)
    exponent = jnp.exp(scores - row_max)
    row_total = jnp.sum(exponent, axis=-1, keepdims=True)
    attn_probs = exponent / row_total
    log_total = row_max + jnp.log(row_total)
    attended = matmul(attn_probs.astype(LOW), value_all, "qk,kd->qd")
    attended_low = attended.reshape(tok_rows, HEADS * HEAD_DIM).astype(LOW)
    attn_proj = matmul(attended_low, out_full, "tq,qc->tc")
    post_val, post_pull = jax.vjp(scaled, attn_proj, gain_post)
    residual = tok_float + post_val
    pre_val, pre_pull = jax.vjp(scaled, residual, gain_pre)
    normed_two = pre_val.astype(LOW)
    both = matmul(normed_two, pair_full, "tc,cf->tf").reshape(tok_rows, spots, 2, ff_cols)
    gate_proj, up_proj = both[:, :, 0], both[:, :, 1]
    mixed_val, mixed_pull = jax.vjp(geglu, gate_proj, up_proj)
    mixed_low = mixed_val.astype(LOW).reshape(tok_rows, ff)
    ffn_proj = matmul(mixed_low, down_full, "tf,fc->tc")
    ffn_val, ffn_pull = jax.vjp(scaled, ffn_proj, gain_ffn)
    block_out = (residual + ffn_val).astype(LOW)

    def halves(array, part):
        split = array.reshape(tok_rows, depth, 2, part)
        keep = take(split, grid.core, 2).reshape(tok_rows, depth * part)
        send = take(split, 1 - grid.core, 2).reshape(tok_rows, depth * part)
        return keep, send

    upstream = cotangent.astype(F32)
    d_ffn_proj, d_gain_ffn = ffn_pull(upstream)
    d_ffn_low = d_ffn_proj.astype(LOW)
    mixed_keep, mixed_send = halves(mixed_low, down_part * spots)
    grad_down = [matmul(m, d_ffn_low, "tf,tc->fc").astype(LOW) for m in (mixed_keep, mixed_send)]
    d_mixed = matmul(d_ffn_low, down_full, "tc,fc->tf").reshape(tok_rows, spots, ff_cols)
    d_gate, d_up = mixed_pull(d_mixed)
    d_both = jnp.stack([d_gate.astype(LOW), d_up.astype(LOW)], axis=2).reshape(tok_rows, 2 * ff)
    two_keep, two_send = halves(normed_two, half)
    grad_pair = [matmul(m, d_both, "tc,tf->cf").astype(LOW) for m in (two_keep, two_send)]
    d_normed_two = matmul(d_both, pair_full, "tf,cf->tc")
    d_resid_part, d_gain_pre = pre_pull(d_normed_two)
    d_residual = upstream + d_resid_part
    d_attn_proj, d_gain_post = post_pull(d_residual)
    d_attn_low = d_attn_proj.astype(LOW)
    att_keep, att_send = halves(attended_low, out_part * spots)
    grad_out = [matmul(m, d_attn_low, "tq,tc->qc").astype(LOW) for m in (att_keep, att_send)]

    pair_keep, pair_send = [
        g.reshape(depth, half, side, side, 2 * ff_cols).transpose(0, 2, 3, 1, 4)
        for g in grad_pair
    ]
    pair_sum = reduce_depth(grid, reduce_plane(grid, pair_keep, pair_send))
    row_keep, row_send = [
        jnp.concatenate(
            [
                o.reshape(depth, side, side, out_part, width),
                d.reshape(depth, side, side, down_part, width),
            ],
            axis=3,
        )
        for o, d in zip(grad_out, grad_down)
    ]
    row_sum = reduce_depth(grid, reduce_plane(grid, row_keep, row_send))

    d_attended = (
        matmul(d_attn_low, out_full, "tc,qc->tq")
        .astype(LOW)
        .reshape(tok_rows * HEADS, HEAD_DIM)
    )
    scores_again = attend_scores(queries, key_all, allowed)
    probs_again = jnp.exp(scores_again - log_total)
    d_values_all = matmul(probs_again.astype(LOW), d_attended, "qk,qd->kd")
    d_probs = matmul(d_attended, value_all, "qd,kd->qk")
    d_scores = probs_again * (d_probs - jnp.sum(d_probs * probs_again, axis=-1, keepdims=True))
    d_scores_low = d_scores.astype(LOW)
    d_keys_all = matmul(d_scores_low, queries, "qk,qd->kd") * HEAD_DIM ** (-0.5)
    d_kv_all = jnp.concatenate([d_keys_all, d_values_all], axis=1)
    near_back = shifted(d_kv_all[tok_rows : 2 * tok_rows].astype(LOW), -1)
    far_back = shifted(d_kv_all[:tok_rows].astype(LOW), -2)
    d_queries = matmul(d_scores_low, key_all, "qk,kd->qd") * HEAD_DIM ** (-0.5)
    d_q_proj, d_gain_query = query_pull(d_queries.reshape(tok_rows, HEADS, HEAD_DIM))
    d_kv = add_low(d_kv_all[2 * tok_rows :], near_back, far_back)
    d_k_proj, d_gain_key = key_pull(d_kv[:, :kd])
    d_proj = jnp.concatenate(
        [d_q_proj.astype(LOW), d_k_proj.astype(LOW), d_kv[:, kd:].astype(LOW)], axis=1
    )
    in_keep, in_send = halves(normed_low, half)
    grad_proj = [matmul(m, d_proj, "tc,tq->cq").astype(LOW) for m in (in_keep, in_send)]
    d_normed = matmul(d_proj, proj_full, "tq,cq->tc")
    d_tok_part, d_gain_in = in_pull(d_normed)
    tokens_grad = (d_residual + d_tok_part).astype(LOW)

    proj_keep, proj_send = [
        g.reshape(depth, half, side, side, proj_cols).transpose(0, 2, 3, 1, 4)
        for g in grad_proj
    ]
    proj_sum = reduce_depth(grid, reduce_plane(grid, proj_keep, proj_send))

    d_gains = [d_gain_in, d_gain_post, d_gain_pre, d_gain_ffn, d_gain_query, d_gain_key]
    d_all = jnp.concatenate([g.reshape(depth, -1) for g in d_gains], axis=1)
    lanes = 128
    pad = -(-gain_len // lanes) * lanes - gain_len
    d_all = jnp.pad(d_all, ((0, 0), (0, pad))).reshape(depth, -1, lanes)
    d_all = add_low(d_all, grid.over_core(d_all.astype(LOW)))
    low_all = d_all.astype(LOW)
    d_all = add_low(d_all, *[grid.over_first(low_all, k) for k in range(1, side)])
    low_all = d_all.astype(LOW)
    d_all = add_low(d_all, *[grid.over_second(low_all, k) for k in range(1, side)])
    gain_total = reduce_depth(grid, d_all.astype(LOW)).reshape(-1)
    gain_outs = [gain_total[s : s + n] for s, n in zip(gain_starts, gain_sizes)]

    def whole(block):
        return jnp.stack(gather_core(grid, gather_plane(grid, block.astype(LOW))))

    pair_out = whole(pair_sum).transpose(0, 3, 1, 2, 4).reshape(rows, spots, 2, ff_cols)
    pair_out = pair_out.astype(F32)
    total_gate = pair_out[:, :, 0].reshape(rows, ff)
    total_up = pair_out[:, :, 1].reshape(rows, ff)
    row_out = whole(row_sum).astype(F32)
    total_out = row_out[:, :, :, :out_part].reshape(out_rows, width)
    total_down = row_out[:, :, :, out_part:].reshape(down_rows, width)
    proj_out = whole(proj_sum).transpose(0, 3, 1, 2, 4).reshape(rows, qd + 2 * kd).astype(F32)
    return (
        block_out,
        tokens_grad,
        proj_out[:, :qd],
        proj_out[:, qd : qd + kd],
        proj_out[:, qd + kd :],
        total_out,
        total_gate,
        total_up,
        total_down,
        gain_outs[0],
        gain_outs[4],
        gain_outs[5],
        gain_outs[1],
        gain_outs[2],
        gain_outs[3],
    )


STEPS = ((0, 0), (1, 0), (0, 1), (1, 1))
FLIPS = (0, 2, 1, 3)
NT = (((1,), (1,)), ((), ()))
TN = (((0,), (0,)), ((), ()))
NN = (((1,), (0,)), ((), ()))
GELU_A = math.sqrt(2.0 / math.pi)
GELU_B = 0.044715


def dot(left, right, dims=NN):
    return lax.dot_general(left, right, dims, preferred_element_type=F32)


def spot_of(co, core_side, step):
    core, first, second = co[1], co[2], co[3]
    if core_side == 0:
        half, b1, b2 = core, first, second
    else:
        half, b1, b2 = 1 - core, second, first
    b1 = lax.rem(b1 + step[0], 2)
    b2 = lax.rem(b2 + step[1], 2)
    return half, 2 * b2 + b1


def each_piece(co, refs):
    for side in range(2):
        for i, step in enumerate(STEPS):
            half, place = spot_of(co, side, step)
            yield refs[4 * side + i], half, place


def at_rows(start, size, tile=16):
    return pl.ds(pl.multiple_of(start, tile), size)


def run_all(copies):
    for copy in copies:
        copy.start()


def wait_all(copies):
    for copy in copies:
        copy.wait()


def root_of(v):
    return lax.rsqrt(jnp.mean(v * v, axis=-1, keepdims=True) + EPS)


def norm_back(v, root, gain_one, dy):
    u = dy * gain_one
    dv = root * u - v * (root * root * root) * jnp.mean(u * v, axis=-1, keepdims=True)
    return dv, jnp.sum(dy * v * root, axis=0, keepdims=True)


def turn(v, cos, sin):
    h = v.shape[-1] // 2
    a, b = v[:, :h], v[:, h:]
    return jnp.concatenate([a * cos - b * sin, b * cos + a * sin], axis=-1)


def turn_back(v, cos, sin):
    h = v.shape[-1] // 2
    a, b = v[:, :h], v[:, h:]
    return jnp.concatenate([a * cos + b * sin, b * cos - a * sin], axis=-1)


VM = pl.BlockSpec(memory_space=pltpu.VMEM)
SM = pl.BlockSpec(memory_space=pltpu.SMEM)
AN = pl.BlockSpec(memory_space=pl.ANY)


GRANT = {
    "pk": 60,
    "at": 60,
    "ff": 60,
    "ab": 20,
    "qb": 10,
    "pb": 16,
    "u0": 12,
    "u1": 12,
    "ur": 10,
    "up": 8,
}


def call(kernel, outs, ins, args, scratch, name, flops, moved, aliases=None):
    made = pl.pallas_call(
        kernel,
        out_shape=[jax.ShapeDtypeStruct(s, d) for s, d, _ in outs],
        in_specs=ins,
        out_specs=[m for _, _, m in outs],
        scratch_shapes=scratch,
        input_output_aliases=aliases or {},
        cost_estimate=pl.CostEstimate(flops=flops, bytes_accessed=moved, transcendentals=0),
        compiler_params=pltpu.CompilerParams(vmem_limit_bytes=GRANT[name] * 1024 * 1024),
    )
    return made(*args)


def pack_kernel(
    co, w_query, w_key, w_value, w_out, w_down, w_gate, w_up, proj_o, row_o, pair_o,
    sems, sem,
):
    core, place = co[1], 2 * co[3] + co[2]
    half, cols = w_query.shape[0] // 2, proj_o.shape[1]
    ff_cols = pair_o.shape[1] // 2
    out_part = w_out.shape[0] // 8
    down_part = w_down.shape[0] // 8
    rows = at_rows(core * half, half)
    spot = core * 4 + place
    copies = [
        (w_out.at[at_rows(spot * out_part, out_part)], row_o.at[pl.ds(0, out_part)]),
        (w_down.at[at_rows(spot * down_part, down_part)], row_o.at[pl.ds(out_part, down_part)]),
        (
            w_gate.at[rows, at_rows(place * ff_cols, ff_cols, 128)],
            pair_o.at[:, pl.ds(0, ff_cols)],
        ),
        (
            w_up.at[rows, at_rows(place * ff_cols, ff_cols, 128)],
            pair_o.at[:, pl.ds(ff_cols, ff_cols)],
        ),
    ]
    copies = [pltpu.make_async_copy(s, d, sems.at[i]) for i, (s, d) in enumerate(copies)]
    run_all(copies)
    for p in range(4):

        @pl.when(place == p)
        def _():
            start, found = 0, []
            for w in (w_query, w_key, w_value):
                low = max(p * cols, start)
                high = min((p + 1) * cols, start + w.shape[1])
                if low < high:
                    found.append(
                        pltpu.make_async_copy(
                            w.at[rows, pl.ds(low - start, high - low)],
                            proj_o.at[:, pl.ds(low - p * cols, high - low)],
                            sem,
                        )
                    )
                start += w.shape[1]
            run_all(found)
            wait_all(found)

    wait_all(copies)


def gains_of(co, blocks, rows, thin_rows, width, thin_width):
    lanes = blocks[0].shape[1]
    wide, thin = 0.0, 0.0
    for k, block in enumerate(blocks):
        shard = co[0] ^ k
        values = block[...]
        for n, total in ((rows, width), (thin_rows, thin_width)):
            lane = lax.broadcasted_iota(jnp.int32, (lanes, total), 0)
            spot = lax.broadcasted_iota(jnp.int32, (lanes, total), 1) - shard * n
            pick = jnp.where((lane == spot) & (lane < n), 1.0, 0.0).astype(LOW)
            part = dot(values, pick)
            if total == width:
                wide = wide + part
            else:
                thin = thin + part
    return wide, thin


def attend_kernel(
    co, tok, near, far, own_block, block_1, block_2, block_3, cos, sin, bias,
    w_query, w_key, w_value, *rest,
):
    pieces = rest[:8]
    normed_o, proj_o, key_proj_o, queries_o, keys_o, values_o = rest[8:14]
    attended_o, lse_o, w_o, gains, sem = rest[14:]
    z = co[0]
    n = tok.shape[0]
    rows, qd = w_query.shape
    kd = w_key.shape[1]
    half = rows // 2
    cols = pieces[0].shape[2]
    own = at_rows(z * rows, rows)
    copies = [
        (w_query, w_o.at[own, pl.ds(0, qd)]),
        (w_key, w_o.at[own, pl.ds(qd, kd)]),
        (w_value, w_o.at[own, pl.ds(qd + kd, kd)]),
    ]
    for ref, side, place in each_piece(co, pieces):
        for k in range(3):
            shard = z ^ (k + 1)
            copies.append(
                (
                    ref.at[k],
                    w_o.at[
                        at_rows(shard * rows + side * half, half),
                        at_rows(place * cols, cols, 128),
                    ],
                )
            )
    copies = [pltpu.make_async_copy(s, d, sem) for s, d in copies]
    run_all(copies)
    blocks = (own_block, block_1, block_2, block_3)
    wide, thin = gains_of(co, blocks, rows, kd // 4, tok.shape[1], kd)
    gains[...] = wide
    gains[4:6, :kd] = thin[4:6, :]
    gain_in = 1.0 + gains[0:1, :]
    gain_query = 1.0 + gains[4:5, :HEAD_DIM]
    gain_key = 1.0 + gains[5:6, :HEAD_DIM]

    def normed_of(ref):
        v = ref[...].astype(F32)
        return (v * root_of(v) * gain_in).astype(LOW)

    low = normed_of(tok)
    normed_o[...] = low
    halo = [normed_of(far), normed_of(near)]
    wait_all(copies)
    proj = dot(low, w_o[...])
    proj_o[...] = proj[:, :qd]
    key_proj_o[...] = proj[:, qd : qd + kd]
    for i in range(3):
        kv = proj[:, qd:] if i == 2 else dot(halo[i], w_o[:, qd:])
        at = slice(i * n, (i + 1) * n)
        k = kv[:, :kd]
        k = turn(k * root_of(k) * gain_key, cos[at, :], sin[at, :])
        keys_o[at, :] = k.astype(LOW)
        values_o[at, :] = kv[:, kd:].astype(LOW)
    own_cos, own_sin = cos[2 * n :, :], sin[2 * n :, :]
    for h in range(HEADS):
        at = slice(h * HEAD_DIM, (h + 1) * HEAD_DIM)
        q = proj[:, at]
        q = turn(q * root_of(q) * gain_query, own_cos, own_sin).astype(LOW)
        queries_o[:, at] = q
        scores = dot(q, keys_o[...], NT) * HEAD_DIM ** (-0.5) + bias[...]
        top = jnp.max(scores, axis=-1, keepdims=True)
        e = jnp.exp(scores - top)
        total = jnp.sum(e, axis=-1, keepdims=True)
        p = e / total
        lse_o[h] = jnp.broadcast_to(top + jnp.log(total), lse_o.shape[1:])
        attended_o[:, at] = dot(p.astype(LOW), values_o[...]).astype(LOW)


def out_copies(co, grad, row_of, size, cols_of, refs, sem, dst_rows=None):
    z = co[0]
    found = []
    for side in range(2):
        late, mid, last = refs[3 * side : 3 * side + 3]
        for step in STEPS:
            half, place = spot_of(co, side, step)
            for k, flip in enumerate(FLIPS):
                shard = z ^ flip
                target = late.at[step[1], k] if step[0] else (mid if step[1] else last).at[k]
                if dst_rows is not None:
                    target = target.at[dst_rows]
                source = grad
                if row_of is not None:
                    source = grad.at[at_rows(row_of(shard, half, place), size)]
                    if cols_of is not None:
                        width = cols_of
                        source = grad.at[
                            at_rows(row_of(shard, half, place), size),
                            at_rows(place * width, width, 128),
                        ]
                found.append(pltpu.make_async_copy(source, target, sem))
    return found


def ffn_kernel(co, tok, cot, att, gains, w_out, w_down, w_gate, w_up, *rest):
    row_pieces, pair_pieces = rest[:8], rest[8:16]
    block_o, resid_o, d_att_o, gain_o = rest[16:20]
    pair_refs, row_refs = rest[20:26], rest[26:32]
    (
        out_w,
        down_w,
        pair_w,
        out_g,
        down_g,
        pair_g,
        two_s,
        act_s,
        back_s,
        mixed_s,
        sems,
    ) = rest[32:]
    z = co[0]
    out_rows, down_rows = w_out.shape[0], w_down.shape[0]
    rows, ff = w_gate.shape
    half = rows // 2
    fc = ff // 4
    out_part, down_part = out_rows // 8, down_rows // 8

    def copies_of(pairs, sem):
        return [pltpu.make_async_copy(s, d, sem) for s, d in pairs]

    into_out = [(w_out, out_w.at[at_rows(z * out_rows, out_rows)])]
    into_down = [(w_down, down_w.at[at_rows(z * down_rows, down_rows)])]
    for ref, side, place in each_piece(co, row_pieces):
        for k in range(3):
            shard = z ^ (k + 1)
            spot = side * 4 + place
            into_out.append(
                (
                    ref.at[k, pl.ds(0, out_part)],
                    out_w.at[at_rows(shard * out_rows + spot * out_part, out_part)],
                )
            )
            into_down.append(
                (
                    ref.at[k, pl.ds(out_part, down_part)],
                    down_w.at[at_rows(shard * down_rows + spot * down_part, down_part)],
                )
            )
    into_pair = []
    for q in range(4):
        for i, w in enumerate((w_gate, w_up)):
            into_pair.append(
                (
                    w.at[:, pl.ds(q * fc, fc)],
                    pair_w.at[at_rows(z * rows, rows), pl.ds((2 * q + i) * fc, fc)],
                )
            )
    for ref, side, place in each_piece(co, pair_pieces):
        for k in range(3):
            shard = z ^ (k + 1)
            into_pair.append(
                (
                    ref.at[k],
                    pair_w.at[
                        at_rows(shard * rows + side * half, half),
                        at_rows(place * 2 * fc, 2 * fc, 128),
                    ],
                )
            )
    into_out = copies_of(into_out, sems.at[0])
    into_pair = copies_of(into_pair, sems.at[1])
    into_down = copies_of(into_down, sems.at[2])
    run_all(into_out)
    run_all(into_pair)
    run_all(into_down)

    gain_post = 1.0 + gains[1:2, :]
    gain_pre = 1.0 + gains[2:3, :]
    gain_ffn = 1.0 + gains[3:4, :]
    wait_all(into_out)
    attn = dot(att[...], out_w[...])
    attn_root = root_of(attn)
    residual = tok[...].astype(F32) + attn * attn_root * gain_post
    res_root = root_of(residual)
    two_s[...] = (residual * res_root * gain_pre).astype(LOW)
    wait_all(into_pair)
    wait_all(into_down)
    ffn = None
    for q in range(4):
        both = dot(two_s[...], pair_w[:, 2 * q * fc : 2 * (q + 1) * fc])
        gate, up = both[:, :fc], both[:, fc:]
        t = jnp.tanh(GELU_A * (gate + GELU_B * gate * gate * gate))
        act = 0.5 * gate * (1.0 + t)
        slope = 0.5 * (1.0 + t) + 0.5 * gate * (1.0 - t * t) * (
            GELU_A * (1.0 + 3.0 * GELU_B * gate * gate)
        )
        at = slice(q * fc, (q + 1) * fc)
        act_s[:, at] = act
        back_s[:, at] = up * slope
        mixed = (act * up).astype(LOW)
        mixed_s[:, at] = mixed
        part = dot(mixed, down_w[at, :])
        ffn = part if ffn is None else ffn + part
    ffn_root = root_of(ffn)
    block_o[...] = (residual + ffn * ffn_root * gain_ffn).astype(LOW)

    upstream = cot[...].astype(F32)
    d_ffn, d_gain_ffn = norm_back(ffn, ffn_root, gain_ffn, upstream)
    d_ffn = d_ffn.astype(LOW)
    d_two = None
    for q in range(4):
        at = slice(q * fc, (q + 1) * fc)
        d_mixed = dot(d_ffn, down_w[at, :], NT)
        down_g[at, :] = dot(mixed_s[:, at], d_ffn, TN).astype(LOW)
        d_both = jnp.concatenate(
            [d_mixed * back_s[:, at], d_mixed * act_s[:, at]], axis=1
        ).astype(LOW)
        wide = slice(2 * q * fc, 2 * (q + 1) * fc)
        pair_g[:, wide] = dot(two_s[...], d_both, TN).astype(LOW)
        part = dot(d_both, pair_w[:, wide], NT)
        d_two = part if d_two is None else d_two + part
    pair_copies = out_copies(
        co,
        pair_g,
        lambda shard, side, place: shard * rows + side * half,
        half,
        2 * fc,
        pair_refs,
        sems.at[3],
    )
    down_copies = out_copies(
        co,
        down_g,
        lambda shard, side, place: shard * down_rows + (side * 4 + place) * down_part,
        down_part,
        None,
        row_refs,
        sems.at[4],
        pl.ds(out_part, down_part),
    )
    run_all(pair_copies)
    run_all(down_copies)
    d_res, d_gain_pre = norm_back(residual, res_root, gain_pre, d_two)
    d_res = upstream + d_res
    resid_o[...] = d_res
    d_attn, d_gain_post = norm_back(attn, attn_root, gain_post, d_res)
    d_attn = d_attn.astype(LOW)
    out_g[...] = dot(att[...], d_attn, TN).astype(LOW)
    outer_copies = out_copies(
        co,
        out_g,
        lambda shard, side, place: shard * out_rows + (side * 4 + place) * out_part,
        out_part,
        None,
        row_refs,
        sems.at[5],
        pl.ds(0, out_part),
    )
    run_all(outer_copies)
    d_att_o[...] = dot(d_attn, out_w[...], NT).astype(LOW)
    gain_o[0:1, :] = d_gain_post
    gain_o[1:2, :] = d_gain_pre
    gain_o[2:3, :] = d_gain_ffn
    gain_o[3:, :] = jnp.zeros_like(gain_o[3:, :])
    wait_all(pair_copies)
    wait_all(down_copies)
    wait_all(outer_copies)


def attend_back_kernel(
    queries, keys, values, d_att, lse, bias, proj, cos, sin, gains,
    d_query_o, near_o, far_o, own_o, gain_o, d_keys, d_values,
):
    n = queries.shape[0]
    kd = keys.shape[1]
    unit = HEAD_DIM ** (-0.5)
    gain_query = 1.0 + gains[4:5, :HEAD_DIM]
    own_cos, own_sin = cos[2 * n :, :], sin[2 * n :, :]
    gain_sum = None
    for h in range(HEADS):
        at = slice(h * HEAD_DIM, (h + 1) * HEAD_DIM)
        q, da = queries[:, at], d_att[:, at]
        scores = dot(q, keys[...], NT) * unit + bias[...]
        p = jnp.exp(scores - lse[h][:, :1])
        d_p = dot(da, values[...], NT)
        d_s = (p * (d_p - jnp.sum(d_p * p, axis=-1, keepdims=True))).astype(LOW)
        d_v = dot(p.astype(LOW), da, TN)
        d_k = dot(d_s, q, TN)
        if h == 0:
            d_values[...] = d_v
            d_keys[...] = d_k
        else:
            d_values[...] += d_v
            d_keys[...] += d_k
        d_q = turn_back(dot(d_s, keys[...]) * unit, own_cos, own_sin)
        v = proj[:, at]
        d_v_q, d_gain = norm_back(v, root_of(v), gain_query, d_q)
        d_query_o[:, at] = d_v_q.astype(LOW)
        gain_sum = d_gain if gain_sum is None else gain_sum + d_gain
    gain_o[...] = jnp.broadcast_to(gain_sum, gain_o.shape)
    for ref, start in ((far_o, 0), (near_o, n), (own_o, 2 * n)):
        ref[:, :kd] = (d_keys[start : start + n, :] * unit).astype(ref.dtype)
        ref[:, kd:] = d_values[start : start + n, :].astype(ref.dtype)


def query_back_kernel(d_query, normed, w, grad_o, part_o):
    grad_o[...] = dot(normed[...], d_query[...], TN).astype(LOW)
    part_o[...] = dot(d_query[...], w[:, : d_query.shape[1]], NT)


def proj_back_kernel(
    co, own, near, far, key_proj, cos, sin, gains, query_part, normed, tok, d_res, ffn_gains,
    q_gain, w, query_grad, tokens_o, *rest,
):
    refs, (grad, low_tail, tail, w_kv, sems) = rest[:6], rest[6:]
    n, width = tok.shape
    kd = key_proj.shape[1]
    qd = query_grad.shape[1]
    rows = w.shape[0] // 4
    half = rows // 2
    cols = w.shape[1] // 4
    loads = [
        pltpu.make_async_copy(w.at[:, pl.ds(qd, 2 * kd)], w_kv, sems.at[2]),
        pltpu.make_async_copy(query_grad, grad.at[:, pl.ds(0, qd)], sems.at[3]),
    ]
    run_all(loads)
    d_kv = own[...] + near[...].astype(F32) + far[...].astype(F32)
    gain_key = 1.0 + gains[5:6, :kd]
    gain_in = 1.0 + gains[0:1, :]
    v = key_proj[...]
    d_k = turn_back(d_kv[:, :kd], cos[2 * n :, :], sin[2 * n :, :])
    d_k, d_gain_key = norm_back(v, root_of(v), gain_key, d_k)
    d_proj = jnp.concatenate([d_k.astype(LOW), d_kv[:, kd:].astype(LOW)], axis=1)
    grad[:, qd:] = dot(normed[...], d_proj, TN).astype(LOW)
    wait_all(loads)
    copies = out_copies(
        co,
        grad,
        lambda shard, side, place: shard * rows + side * half,
        half,
        cols,
        refs,
        sems.at[0],
        pl.ds(0, half),
    )
    run_all(copies)
    d_normed = query_part[...] + dot(d_proj, w_kv[...], NT)
    x = tok[...].astype(F32)
    d_x, d_gain_in = norm_back(x, root_of(x), gain_in, d_normed)
    tokens_o[...] = (d_res[...] + d_x).astype(LOW)
    tail[...] = jnp.zeros_like(tail)
    parts = [d_gain_in, ffn_gains[0:1, :], ffn_gains[1:2, :], ffn_gains[2:3, :]]
    for i, part in enumerate(parts):
        tail[2 * i : 2 * i + 1, :] = part[:, :cols]
        tail[2 * i + 1 : 2 * i + 2, : width - cols] = part[:, cols:]
    tail[8:9, :kd] = q_gain[0:1, :]
    tail[9:10, :kd] = d_gain_key
    low_tail[...] = tail[...].astype(LOW)
    tail_rows = low_tail.shape[0]
    more = out_copies(
        co, low_tail, None, None, None, refs, sems.at[1], pl.ds(half, tail_rows)
    )
    run_all(more)
    wait_all(copies)
    wait_all(more)


def unpack_pair_kernel(core_side, co, *rest):
    pieces = rest[:4]
    gate_o, up_o, wide, sem = rest[-4:]
    half = gate_o.shape[0] // 2
    fc = gate_o.shape[1] // 4
    copies = []
    for i, step in enumerate(STEPS):
        side, place = spot_of(co, core_side, step)
        wide[i] = pieces[i][...].astype(F32)
        at = (at_rows(side * half, half), at_rows(place * fc, fc, 128))
        found = [
            pltpu.make_async_copy(wide.at[i, :, pl.ds(0, fc)], gate_o.at[at], sem),
            pltpu.make_async_copy(wide.at[i, :, pl.ds(fc, fc)], up_o.at[at], sem),
        ]
        run_all(found)
        copies += found
    wait_all(copies)


def unpack_row_kernel(co, *rest):
    pieces, (out_o, down_o) = rest[:8], rest[8:]
    out_part, down_part = out_o.shape[0] // 8, down_o.shape[0] // 8
    for ref, side, place in each_piece(co, pieces):
        spot = side * 4 + place
        out_o[at_rows(spot * out_part, out_part), :] = ref[:out_part, :].astype(F32)
        down_o[at_rows(spot * down_part, down_part), :] = ref[out_part:, :].astype(F32)


def unpack_proj_kernel(co, *rest):
    pieces, (query_o, key_o, value_o, tail_o, full) = rest[:8], rest[8:]
    half = query_o.shape[0] // 2
    cols = full.shape[1] // 4
    qd, kd = query_o.shape[1], key_o.shape[1]
    for ref, side, place in each_piece(co, pieces):
        full[at_rows(side * half, half), at_rows(place * cols, cols, 128)] = ref[
            :half, :
        ].astype(F32)
    query_o[...] = full[:, :qd]
    key_o[...] = full[:, qd : qd + kd]
    value_o[...] = full[:, qd + kd :]
    tail_o[...] = pieces[0][half:, :].astype(F32)


def spread(grid, block, wait=()):
    own = [block]
    own.append(grid.over_first(block, 1))
    own.append(grid.over_second(block, 1))
    own.append(grid.over_second(own[1], 1))
    sent = own[:2] + [after(own[2], *wait) if wait else own[2]] + own[3:]
    return own + [grid.over_core(b) for b in sent]


def along_depth(grid, block):
    two = grid.over_flip(block, 2)
    one = grid.over_flip(block, 1)
    return [one, two, grid.over_flip(two, 1)]


def after(value, *others):
    return lax.optimization_barrier((value, *others))[0]


def first_sum(grid, arrays, wait=()):
    keep_late, keep_mid, keep_last, send_late, send_mid, send_last = arrays
    late_got = grid.over_core(send_late)
    mid_got = grid.over_core(send_mid)
    last_got = grid.over_core(send_last)
    if wait:
        keep_late = after(keep_late, *wait)
    late = add_low(keep_late, late_got).astype(LOW)
    first_got = grid.over_first(late, 1)
    return (keep_last, last_got, first_got[0]), (keep_mid, mid_got, first_got[1])


def second_sum(begun, wait=()):
    parts, (keep_mid, mid_got, first_got) = begun
    if wait:
        keep_mid = after(keep_mid, *wait)
    return parts, add_low(keep_mid, mid_got, first_got).astype(LOW)


def plane_sums(grid, begun, wait=()):
    parts, mid = begun
    parts = (*parts, grid.over_second(mid, 1))
    if wait:
        parts = (after(parts[0], *wait), *parts[1:])
    return parts, add_low(*[p[2:] for p in parts]).astype(LOW)


def depth_sum(grid, sums):
    parts, away = sums
    got = grid.over_flip(away, 1)
    far = add_low(*[p[1] for p in parts], got[1]).astype(LOW)
    far_got = grid.over_flip(far, 2)
    return add_low(*[p[0] for p in parts], got[0], far_got).astype(LOW)


def local_fast(
    tokens,
    cotangent,
    seq_lengths,
    w_query,
    w_key,
    w_value,
    w_out,
    w_gate,
    w_up,
    w_down,
    g_in,
    g_query,
    g_key,
    g_post,
    g_pre,
    g_ffn,
):
    grid = Grid()
    n, width = tokens.shape
    rows, qd = w_query.shape
    kd = w_key.shape[1]
    half = rows // 2
    out_rows, down_rows, ff = w_out.shape[0], w_down.shape[0], w_gate.shape[1]
    total_cols = qd + 2 * kd
    cols, fc = total_cols // 4, ff // 4
    out_part, down_part = out_rows // 8, down_rows // 8
    row_part = out_part + down_part
    coords = jnp.stack([grid.z, grid.core, grid.first, grid.second]).astype(jnp.int32)
    dma = pltpu.SemaphoreType.DMA

    proj_mine, row_mine, pair_mine = call(
        pack_kernel,
        [
            ((half, cols), LOW, VM),
            ((row_part, width), LOW, VM),
            ((half, 2 * fc), LOW, VM),
        ],
        [SM] + [AN] * 7,
        (coords, w_query, w_key, w_value, w_out, w_down, w_gate, w_up),
        [dma((4,)), dma],
        "pk",
        0,
        2_000_000,
    )
    device = lax.axis_index(ALL)
    seq_lengths = after(seq_lengths, proj_mine)
    glob_index = device * n + jnp.arange(-2 * n, n, dtype=jnp.int32)
    segment, position = places(glob_index, seq_lengths)
    own_glob = glob_index[2 * n :]
    own_seg = segment[2 * n :]
    cos, sin = turning(position, HEAD_DIM)
    allowed = (
        (segment[None, :] == own_seg[:, None])
        & (glob_index[None, :] <= own_glob[:, None])
        & (own_glob[:, None] - glob_index[None, :] < WINDOW)
        & (glob_index[None, :] >= 0)
    )
    bias = jnp.where(allowed, 0.0, NEGATIVE).astype(F32)

    gains_late = after((g_in, g_post, g_pre, g_ffn, g_query, g_key), proj_mine)
    gain_block = jnp.zeros((16, cols), LOW)
    for i, g in enumerate(gains_late):
        gain_block += jnp.pad(g[None], ((i, 15 - i), (0, cols - g.shape[0])))
    gain_got = [grid.over_flip(gain_block, k) for k in range(1, grid.depth)]
    tokens_late = lax.optimization_barrier((tokens, proj_mine))[0]
    proj_got = along_depth(grid, proj_mine)
    row_got = along_depth(grid, row_mine)
    pair_got = along_depth(grid, pair_mine)
    near_tok = shifted(tokens_late, 1)
    far_tok = shifted(after(near_tok, bias), 1)
    proj_pieces = spread(grid, jnp.stack(proj_got))
    row_pieces = spread(grid, jnp.stack(row_got), (cos, sin))
    pair_pieces = spread(grid, jnp.stack(pair_got))

    normed, proj, key_proj, queries, keys, values, attended, lse, w_full, gains = call(
        attend_kernel,
        [
            ((n, width), LOW, VM),
            ((n, qd), F32, VM),
            ((n, kd), F32, VM),
            ((n, qd), LOW, VM),
            ((3 * n, kd), LOW, VM),
            ((3 * n, kd), LOW, VM),
            ((n, qd), LOW, VM),
            ((HEADS, n, 128), F32, VM),
            ((4 * rows, total_cols), LOW, VM),
            ((16, width), F32, VM),
        ],
        [SM] + [VM] * 10 + [AN] * 11,
        (
            coords, tokens, near_tok, far_tok, gain_block, *gain_got, cos, sin, bias,
            w_query, w_key, w_value, *proj_pieces,
        ),
        [dma],
        "at",
        1_700_000_000,
        9_000_000,
    )

    six = lambda r, c: [
        (((2, 4, r, c) if i == 0 else (4, r, c)), LOW, AN) for i in (0, 1, 2, 0, 1, 2)
    ]
    found = call(
        ffn_kernel,
        [
            ((n, width), LOW, VM),
            ((n, width), F32, VM),
            ((n, qd), LOW, VM),
            ((8, width), F32, VM),
        ]
        + six(half, 2 * fc)
        + six(row_part, width),
        [SM] + [VM] * 4 + [AN] * 20,
        (
            coords, tokens, cotangent, attended, gains,
            w_out, w_down, w_gate, w_up, *row_pieces, *pair_pieces,
        ),
        [
            pltpu.VMEM((4 * out_rows, width), LOW),
            pltpu.VMEM((4 * down_rows, width), LOW),
            pltpu.VMEM((4 * rows, 2 * ff), LOW),
            pltpu.VMEM((4 * out_rows, width), LOW),
            pltpu.VMEM((4 * down_rows, width), LOW),
            pltpu.VMEM((4 * rows, 2 * ff), LOW),
            pltpu.VMEM((n, width), LOW),
            pltpu.VMEM((n, ff), F32),
            pltpu.VMEM((n, ff), F32),
            pltpu.VMEM((n, ff), LOW),
            dma((6,)),
        ],
        "ff",
        7_000_000_000,
        20_000_000,
    )
    block_out, d_res, d_att, ffn_gains = found[:4]
    pair_late = first_sum(grid, found[4:10])
    row_late = first_sum(grid, found[10:16])
    d_query, near_d, far_d, own_d, q_gain = call(
        attend_back_kernel,
        [
            ((n, qd), LOW, VM),
            ((n, 2 * kd), LOW, VM),
            ((n, 2 * kd), LOW, VM),
            ((n, 2 * kd), F32, VM),
            ((8, kd), F32, VM),
        ],
        [VM] * 10,
        (queries, keys, values, d_att, lse, bias, proj, cos, sin, gains),
        [pltpu.VMEM((3 * n, kd), F32), pltpu.VMEM((3 * n, kd), F32)],
        "ab",
        2_000_000_000,
        7_000_000,
    )
    near_back = shifted(near_d, -1)
    far_back = shifted(far_d, -2)
    query_grad, query_part = call(
        query_back_kernel,
        [((4 * rows, qd), LOW, VM), ((n, width), F32, VM)],
        [VM] * 3,
        (d_query, normed, w_full),
        [],
        "qb",
        700_000_000,
        5_000_000,
    )
    pair_begun = second_sum(pair_late)
    row_begun = second_sum(row_late, (query_part,))
    pair_sums = plane_sums(grid, pair_begun, row_begun[1:])
    row_sums = plane_sums(grid, row_begun)
    pair_sum = depth_sum(grid, pair_sums)
    row_sum = depth_sum(grid, row_sums)
    found = call(
        proj_back_kernel,
        [((n, width), LOW, VM)] + six(half + 16, cols),
        [SM] + [VM] * 13 + [AN] * 2,
        (
            coords, own_d, near_back, far_back, key_proj, cos, sin, gains,
            query_part, normed, tokens, d_res, ffn_gains, q_gain, w_full, query_grad,
        ),
        [
            pltpu.VMEM((4 * rows, total_cols), LOW),
            pltpu.VMEM((16, cols), LOW),
            pltpu.VMEM((16, cols), F32),
            pltpu.VMEM((4 * rows, 2 * kd), LOW),
            dma((4,)),
        ],
        "pb",
        400_000_000,
        6_000_000,
    )
    tokens_grad = found[0]
    proj_begun = second_sum(first_sum(grid, found[1:7]))
    proj_sum = depth_sum(grid, plane_sums(grid, proj_begun))

    pieces = spread(grid, pair_sum)
    made = ()
    for core_side in range(2):
        made = call(
            functools.partial(unpack_pair_kernel, core_side),
            [((rows, ff), F32, AN)] * 2,
            [SM] + [VM] * 4 + [AN] * len(made),
            (coords, *pieces[4 * core_side : 4 * core_side + 4], *made),
            [pltpu.VMEM((4, half, 2 * fc), F32), dma],
            "u" + str(core_side),
            0,
            4_000_000,
            {5 + i: i for i in range(len(made))},
        )
    total_gate, total_up = made
    total_out, total_down = call(
        unpack_row_kernel,
        [((out_rows, width), F32, VM), ((down_rows, width), F32, VM)],
        [SM] + [VM] * 8,
        (coords, *spread(grid, row_sum)),
        [],
        "ur",
        0,
        3_000_000,
    )
    total_query, total_key, total_value, tail = call(
        unpack_proj_kernel,
        [
            ((rows, qd), F32, VM),
            ((rows, kd), F32, VM),
            ((rows, kd), F32, VM),
            ((16, cols), F32, VM),
        ],
        [SM] + [VM] * 8,
        (coords, *spread(grid, proj_sum)),
        [pltpu.VMEM((rows, total_cols), F32)],
        "up",
        0,
        2_000_000,
    )
    wide = tail[:8].reshape(4, 2 * cols)[:, :width]
    wide = lax.dynamic_slice_in_dim(wide, grid.z * rows, rows, 1)
    thin = lax.dynamic_slice_in_dim(tail[8:10, :kd], grid.z * (kd // 4), kd // 4, 1)
    return (
        block_out,
        tokens_grad,
        total_query,
        total_key,
        total_value,
        total_out,
        total_gate,
        total_up,
        total_down,
        wide[0],
        thin[0],
        thin[1],
        wide[1],
        wide[2],
        wide[3],
    )


def local(*args):
    w_query, w_out, w_gate, w_down = args[3], args[6], args[7], args[9]
    depth, reps = lax.axis_size("shard"), lax.axis_size("rep")
    aligned = (
        depth == 4
        and reps == 8
        and w_query.shape[0] % 32 == 0
        and w_out.shape[0] % 128 == 0
        and w_down.shape[0] % 128 == 0
        and w_gate.shape[1] % 512 == 0
    )
    if not aligned:
        return local_plain(*args)
    return local_fast(*args)


def solution(mesh):
    rows, cols, vec = P(ALL, None), P("shard", None), P("shard")
    return jax.shard_map(
        local,
        mesh=mesh,
        in_specs=(rows, rows, P()) + (cols,) * 7 + (vec,) * 6,
        out_specs=(rows, rows) + (cols,) * 7 + (vec,) * 6,
        check_vma=False,
    )
```
